512 devices in a mesh: dp: 128 (over y, x, z_lo, core), strip: 4 (over z_hi).
Axes of the slice: x: 4, y: 8, z: 8 (z_hi: 4, z_lo: 2; z = z_hi * 2 + z_lo), core: 2. Of those that a mesh axis runs over, the one named last changes fastest.
Arguments:
- latents: bfloat16 [128, 4, 320, 128], P('dp', 'strip'), may hold values from -6 to 6
- cotangent: bfloat16 [128, 4, 320, 128], P('dp', 'strip'), may hold values from -16 to 16
- weight: bfloat16 [320, 2880], P('strip'), may hold values from -0.109375 to 0.109375
- master: float32 [512, 2880], P('dp'), may hold values from -0.21875 to 0.21875
- first_moment: float32 [512, 2880], P('dp'), may hold values from -6 to 6
- second_moment: float32 [512, 2880], P('dp'), may hold values from 0.005 to 0.05
- owner_list: int32 [320], replicated, may hold values from 0 to 127, as said below
Outputs:
- output: bfloat16 [128, 4, 320, 128], P('dp', 'strip')
- grad_input: bfloat16 [128, 4, 320, 128], P('dp', 'strip')
- new_weight: bfloat16 [320, 2880], P('strip')
- new_master: float32 [512, 2880], P('dp')
- new_first: float32 [512, 2880], P('dp')
- new_second: float32 [512, 2880], P('dp')
The draws below stay inside these ranges and needn't reach their ends.
Inputs may be any that keep to these rules, and one draw needn't show every extreme that they name: `owner_list`: each of the 128 ranks owns at least one and at most 4 buckets, and some rank owns exactly 4.
All inputs are finite; a program needn't handle non-finite values.
Results may differ from the reference program's by a relative error of at most 0.0033.
Values may be sent and summed in bfloat16 or wider, within the bound.
No kernel may reach another device: no remote copies, remote signals or barrier semaphores. Data moves between devices by JAX's collectives and lax.ppermute only.
A program may use at most 64 MiB of HBM per device.

```python
import math
import jax
import jax.numpy as jnp
from jax import lax

C = 320
WID = 128
IMAGES = 128
HEIGHT = 4
OWNERS = 128
CAP = 4


def draw_owner_list(key, part):
    key_rank = jax.random.fold_in(key, 11)
    key_pick = jax.random.fold_in(key, 12)
    key_order = jax.random.fold_in(key, 13)
    rank_list = jax.random.permutation(key_rank, OWNERS).astype(jnp.int32)
    bucket_order = jax.random.permutation(key_order, C).astype(jnp.int32)
    extra_count = C - CAP - (OWNERS - 1)
    picked = jax.random.permutation(key_pick, (OWNERS - 1) * (CAP - 2))[:extra_count].astype(jnp.int32)
    extra = rank_list[1 + picked // (CAP - 2)]
    leader = jnp.zeros((CAP,), jnp.int32) + rank_list[0]
    values = jnp.concatenate([leader, rank_list[1:], extra.astype(jnp.int32)])
    return jnp.zeros((C,), jnp.int32).at[bucket_order].set(values)


def raised(drawn, rng, source, target, shards_of, factor):
    def block_of(axis_at):
        return (jnp.arange(drawn.shape[axis_at]) // (drawn.shape[axis_at] // shards_of)).reshape((-1,) + (1,) * (drawn.ndim - 1 - axis_at))

    first = jax.random.permutation(rng, shards_of)[block_of(target)]
    second = (block_of(target) + shards_of // 2) % shards_of
    return jnp.where((block_of(source) == first) | (block_of(source) == second), factor * drawn, drawn)


def block_levels(stream_key, shape, cuts, smallest, top_value):
    def one(axis_at, shards_of):
        steps = jax.random.uniform(jax.random.fold_in(jax.random.fold_in(stream_key, 6), axis_at), (shards_of,), jnp.float32, smallest / len(cuts), top_value / len(cuts))
        return jnp.repeat(jnp.exp(steps), shape[axis_at] // shards_of).reshape((-1,) + (1,) * (len(shape) - axis_at - 1))

    factor_of = one(*cuts[0])
    for cut in cuts[1:]:
        factor_of = factor_of * one(*cut)
    return factor_of


def centred(own_key, extent, scale, reach, cuts=(), kind=jnp.bfloat16):
    array = jax.random.normal(own_key, extent, jnp.float32) * scale
    if len(cuts) > 0:
        array = block_levels(own_key, extent, cuts, -0.22, 0.18) * array
    return jnp.clip(array, min=-reach, max=reach).astype(kind)


def gaussian_with(rng, shape, scale, limit, shards, heavy, held_as=jnp.bfloat16):
    array = scale * jax.random.normal(rng, shape, jnp.float32)
    if shards:
        array = array * block_levels(rng, shape, shards, -0.22, 0.18)
    return jnp.clip(raised(array, jax.random.fold_in(rng, 3), *heavy), -limit, limit).astype(held_as)


def setup_inputs(seed: int = 0) -> dict:
    keys = jax.random.split(jax.random.key(seed), 8)
    latents = centred(keys[0], (IMAGES, HEIGHT, C, WID), 1.0, 6.0, ((0, 128), (1, 4)))
    cotangent = gaussian_with(keys[1], (IMAGES, HEIGHT, C, WID), 1.0, 16.0, ((0, 128), (1, 4)), (0, 2, 64, 4.0))
    weight = centred(keys[2], (C, 9 * C), (9 * C) ** -0.5, 0.109375, ((0, 4),))
    master = centred(keys[3], (OWNERS * CAP, 9 * C), 0.015, 0.21875, ((0, 128),), jnp.float32)
    first_moment = centred(keys[4], (OWNERS * CAP, 9 * C), 0.5, 6.0, ((0, 128),), jnp.float32)
    second_moment = jnp.clip(jnp.exp(math.log(0.05) - 2.3025851 * jax.random.uniform(keys[5], (OWNERS * CAP, 9 * C), jnp.float32) ** block_levels(keys[5], (OWNERS * CAP, 9 * C), ((0, 128),), -0.2, 0.2)), 0.005, 0.05)
    owner_list = draw_owner_list(jax.random.fold_in(keys[7], 71), 0)
    return dict(latents=latents, cotangent=cotangent, weight=weight, master=master, first_moment=first_moment, second_moment=second_moment, owner_list=owner_list)


beta_first = 0.9
beta_second = 0.999
learn_rate = 0.01
epsilon = 1e-08
bias_first = 1.0 - 0.9 ** 10
bias_second = 1.0 - 0.999 ** 10

def patches(padded, direction):
    widened = jnp.pad(padded, ((0, 0), (0, 0), (1, 1)))
    height = padded.shape[0] - 2
    across = padded.shape[2]
    pieces = []
    for row_step in (-1, 0, 1):
        for col_step in (-1, 0, 1):
            row_start = 1 + direction * row_step
            col_start = 1 + direction * col_step
            pieces.append(widened[row_start:row_start + height, :, col_start:col_start + across])
    return jnp.concatenate(pieces, axis=1)

def flipped(weight):
    channels = weight.shape[0]
    return weight.reshape(channels, 9, channels).transpose(2, 1, 0).reshape(channels, 9 * channels)

def slot_tables(owner_list, capacity):
    count = owner_list.shape[0]
    same_owner = owner_list[:, None] == owner_list[None, :]
    earlier = jnp.arange(count, dtype=jnp.int32)[None, :] < jnp.arange(count, dtype=jnp.int32)[:, None]
    within = lax.optimization_barrier(jnp.sum((same_owner & earlier).astype(jnp.int32), axis=1)).astype(jnp.int32)
    return (owner_list * capacity + within).astype(jnp.int32)

def adam_update(grads, master, first_moment, second_moment, filled):
    first_new = beta_first * first_moment + (1.0 - beta_first) * grads
    second_new = beta_second * second_moment + (1.0 - beta_second) * grads * grads
    update = learn_rate * (first_new / bias_first) / (jnp.sqrt(second_new / bias_second) + epsilon)
    keep = filled[:, None]
    return (jnp.where(keep, master - update, master), jnp.where(keep, first_new, first_moment), jnp.where(keep, second_new, second_moment))

def reference(latents, cotangent, weight, master, first_moment, second_moment, owner_list):
    weight_float = weight.astype(jnp.float32)
    flipped_float = flipped(weight).astype(jnp.float32)
    row_pad = ((1, 1), (0, 0), (0, 0))

    def image_step(grad_sum, pair):
        pixels, upstream = pair
        pixels_float = pixels.astype(jnp.float32)
        active = jax.nn.silu(pixels_float).astype(jnp.bfloat16)
        forward_cols = patches(jnp.pad(active, row_pad), 1).astype(jnp.float32)
        convolved = jnp.einsum('ok,hkw->how', weight_float, forward_cols)
        output = (pixels_float + convolved).astype(jnp.bfloat16)
        backward_cols = patches(jnp.pad(upstream, row_pad), -1).astype(jnp.float32)
        spread = jnp.einsum('ck,hkw->hcw', flipped_float, backward_cols)
        sigmoid_val = jax.nn.sigmoid(pixels_float)
        derivative = sigmoid_val * (1.0 + pixels_float * (1.0 - sigmoid_val))
        upstream_float = upstream.astype(jnp.float32)
        grad_input = (upstream_float + spread * derivative).astype(jnp.bfloat16)
        grad_sum = grad_sum + jnp.einsum('how,hkw->ok', upstream_float, forward_cols)
        return (grad_sum, (output, grad_input))
    summed, (output, grad_input) = lax.scan(image_step, jnp.zeros((C, 9 * C), jnp.float32), (latents, cotangent))
    gradient = summed / jnp.sqrt(jnp.float32(IMAGES * HEIGHT * WID))
    slot_ids = slot_tables(owner_list, CAP)
    matches = slot_ids[None, :] == jnp.arange(OWNERS * CAP, dtype=jnp.int32)[:, None]
    bucket = lax.optimization_barrier(jnp.sum(jnp.where(matches, jnp.arange(C, dtype=jnp.int32)[None, :], 0), axis=1)).astype(jnp.int32)
    filled = jnp.any(matches, axis=1)
    slot_grad = jnp.where(filled[:, None], gradient[bucket], 0.0)
    new_master, new_first, new_second = adam_update(slot_grad, master, first_moment, second_moment, filled)
    new_weight = new_master[slot_ids].astype(jnp.bfloat16)
    return (output, grad_input, new_weight, new_master, new_first, new_second)
```

```python
import functools
import jax
import jax.numpy as jnp
from jax import lax
from jax.experimental import pallas as pl
from jax.experimental.pallas import tpu as pltpu
from jax.sharding import Mesh, PartitionSpec as P

beta_first = 0.9
beta_second = 0.999
learn_rate = 0.01
epsilon = 1e-08
bias_first = 1.0 - 0.9**10
bias_second = 1.0 - 0.999**10

interpret = False
LANES = 128
RANK_SHAPE = (8, 8, 2)
TERMS = 2
taps = [(dh, dw) for dh in (-1, 0, 1) for dw in (-1, 0, 1)]
f32 = jnp.float32
bf16 = jnp.bfloat16


def call(body, out_shape, scratch=(), scalars=0, inputs=0):
    specs = {}
    if scalars:
        specs["in_specs"] = [pl.BlockSpec(memory_space=pltpu.SMEM)] * scalars + [
            pl.BlockSpec(memory_space=pltpu.VMEM)
        ] * inputs
    return pl.pallas_call(
        body,
        out_shape=out_shape,
        scratch_shapes=scratch,
        interpret=interpret,
        compiler_params=pltpu.CompilerParams(vmem_limit_bytes=20 << 20),
        **specs,
    )


def dot(left, right, left_dim, right_dim):
    return lax.dot_general(
        left, right, (((left_dim,), (right_dim,)), ((), ())), preferred_element_type=f32
    )


def shifted(value):
    lane = lax.broadcasted_iota(jnp.int32, value.shape, 1)
    last = value.shape[1] - 1
    before = jnp.where(lane == 0, 0.0, pltpu.roll(value, 1, 1))
    after = jnp.where(lane == last, 0.0, pltpu.roll(value, last, 1))
    return {-1: before.astype(bf16), 0: value.astype(bf16), 1: after.astype(bf16)}


def fill(cols, rows, load, direction):
    first = load(0)
    count, width = first.shape
    for index, (dh, _) in enumerate(taps):
        for h in range(rows):
            if not 0 <= h + direction * dh < rows:
                cols[index * count : (index + 1) * count, h * width : (h + 1) * width] = jnp.zeros(
                    (count, width), bf16
                )
    for source in range(rows):
        versions = shifted(first if source == 0 else load(source))
        for index, (dh, dw) in enumerate(taps):
            h = source - direction * dh
            if 0 <= h < rows:
                cols[index * count : (index + 1) * count, h * width : (h + 1) * width] = versions[
                    direction * dw
                ]


def activated(gathered, channels, h):
    value = gathered[h, :channels, :].astype(f32)
    return (value / (1.0 + jnp.exp(-value))).astype(bf16).astype(f32)


def pack_body(pixels, upstream, outgoing, arrived):
    strips, channels = outgoing.shape[0], pixels.shape[0]
    copies = []
    for strip in range(strips):
        copies.append((pixels, outgoing.at[strip, :channels, :]))
        copies.append((upstream.at[strip], outgoing.at[strip, channels:, :]))
    copies = [
        pltpu.make_async_copy(source, target, arrived.at[index])
        for index, (source, target) in enumerate(copies)
    ]
    for copy in copies:
        copy.start()
    for copy in copies:
        copy.wait()


def split_body(strip, master, first_moment, second_moment, pieces, *, strips, step):
    state = jnp.concatenate([master[...], first_moment[...], second_moment[...]], axis=0)
    terms = []
    for _ in range(TERMS):
        term = state.astype(bf16).astype(f32)
        terms.append(term)
        state = state - term
    terms = jnp.concatenate(terms, axis=0)
    share = terms.shape[0] // strips
    mine = terms[:share]
    for other in range(1, strips):
        mine = jnp.where(strip[0] == other, terms[other * share : (other + 1) * share], mine)
    groups, height, padded = pieces.shape
    excess = (groups - 1) * step + padded - mine.shape[1]
    mine = jnp.concatenate([mine, jnp.zeros((share, excess), f32)], axis=1)
    mine = jnp.concatenate([mine, jnp.zeros((height - share, mine.shape[1]), f32)], axis=0)
    for group in range(groups):
        pieces[group] = mine[:, group * step : group * step + padded].astype(bf16)


def gradient_body(gathered, pieces, grads, cols, *, channels, step):
    rows = gathered.shape[0]
    quarter = gathered.shape[1] - channels
    fill(cols, rows, functools.partial(activated, gathered, channels), 1)
    whole = len(taps) * channels
    if cols.shape[0] > whole:
        cols[whole:, :] = jnp.zeros((cols.shape[0] - whole, cols.shape[1]), bf16)
    upstream = jnp.concatenate([gathered[h, channels:, :] for h in range(rows)], axis=1)
    groups, _, padded = grads.shape
    for group in range(groups):
        product = dot(upstream, cols[group * step : group * step + padded, :], 1, 1)
        grads[group, :quarter, :] = product.astype(bf16)
        grads[group, quarter:, :] = pieces[group]


def convolution_body(
    strip, gathered, residual, weight, turned, *results, channels
):
    *results, cols, back_cols, whole = results
    rows, quarter, width = residual.shape
    fill(cols, rows, functools.partial(activated, gathered, channels), 1)
    convolved = dot(weight[...], cols[...], 1, 0)
    for h in range(rows):
        whole[h, :quarter, :] = (
            residual[h].astype(f32) + convolved[:, h * width : (h + 1) * width]
        ).astype(bf16)
    fill(back_cols, rows, lambda h: gathered[h, channels:, :].astype(f32), -1)
    spread = dot(turned[...], back_cols[...], 1, 0)
    for h in range(rows):
        whole[h, quarter:, :] = spread[:, h * width : (h + 1) * width].astype(bf16)
    for ahead, result in enumerate(results):
        target = strip[0] + ahead
        result[...] = whole[jnp.where(target >= rows, target - rows, target)]


def collect_body(strip, pixels, upstream, *pieces, quarter):
    *pieces, output, grad_input = pieces
    strips = len(pieces)
    spread = jnp.zeros(pixels.shape, f32)
    for behind, piece in enumerate(pieces):
        source = strip[0] - behind
        source = jnp.where(source < 0, source + strips, source)
        output[pl.ds(pl.multiple_of(source * quarter, quarter), quarter), :] = piece[:quarter, :]
        spread = spread + piece[quarter:, :].astype(f32)
    value = pixels[...].astype(f32)
    sigmoid = 1.0 / (1.0 + jnp.exp(-value))
    derivative = sigmoid * (1.0 + value * (1.0 - sigmoid))
    grad_input[...] = (upstream[...].astype(f32) + spread * derivative).astype(bf16)


def turn_body(received, message, *, quarter, share):
    groups, _, padded = received.shape
    values = [received[group].astype(f32) for group in range(groups)]
    total = values[0][:quarter]
    for value in values[1:]:
        total = total + value[:quarter]
    rows = [total] + [value[quarter : quarter + share] for value in values]
    spare = LANES - quarter - groups * share
    if spare:
        rows.append(jnp.zeros((spare, padded), f32))
    turned = jnp.transpose(jnp.concatenate(rows, axis=0))
    parts, strips, chunk, _ = message.shape
    for part in range(parts):
        piece = turned[part * chunk : (part + 1) * chunk, :].astype(bf16)
        for strip in range(strips):
            message[part, strip] = piece


def adam(grads, master, first_moment, second_moment):
    first_new = beta_first * first_moment + (1.0 - beta_first) * grads
    second_new = beta_second * second_moment + (1.0 - beta_second) * grads * grads
    update = learn_rate * (first_new / bias_first) / (jnp.sqrt(second_new / bias_second) + epsilon)
    return master - update, first_new, second_new


def publish_body(
    strip, received, slots, message, *, quarter, capacity, share, groups, cores, root
):
    pairs, chunk, _ = received.shape
    strips = slots.shape[0]
    parts = pairs // strips
    chips = message.shape[0]
    columns = max(LANES, chips * cores * capacity)
    mine = slots[0:1, :]
    for other in range(1, strips):
        mine = jnp.where(strip[0] == other, slots[other : other + 1, :], mine)
    wide = jnp.concatenate([mine] * 3, axis=1)
    owner, place = wide // capacity, wide % capacity
    owner_part = owner // (groups * cores) * cores + owner % cores
    owner_group = owner // cores % groups
    row = lax.broadcasted_iota(jnp.int32, (LANES, 3 * LANES), 0) - quarter
    array = lax.broadcasted_iota(jnp.int32, (LANES, 3 * LANES), 1) // LANES
    usable = (row >= 0) & (row < groups * share) & (row // share == owner_group) & (wide >= 0)
    index = lax.broadcasted_iota(jnp.int32, (columns, LANES), 0)
    chosen = jnp.zeros((chunk, columns), f32)
    grads = jnp.zeros((chunk, LANES), f32)
    picked = jnp.zeros((parts * chunk, 3 * LANES), f32)
    for other in range(strips):
        values = [received[part * strips + other].astype(f32) for part in range(parts)]
        total = values[0]
        for value in values[1:]:
            total = total + value
        matches = jnp.where(index == slots[other : other + 1, :], 1.0, 0.0).astype(bf16)
        chosen = chosen + dot(total.astype(bf16), matches, 1, 1)
        grads = jnp.where(strip[0] == other, total, grads)
        place_of = (other * share + row % share) % (3 * capacity)
        here = usable & (place_of // capacity == array) & (place_of % capacity == place)
        here = jnp.where(here, 1.0, 0.0).astype(bf16)
        picked = picked + dot(jnp.concatenate(values, axis=0).astype(bf16), here, 1, 0)
    state = jnp.zeros((chunk, 3 * LANES), f32)
    for part in range(parts):
        state = state + jnp.where(
            owner_part == part, picked[part * chunk : (part + 1) * chunk], 0.0
        )
    fresh, _, _ = adam(
        grads / root, state[:, :LANES], state[:, LANES : 2 * LANES], state[:, 2 * LANES :]
    )
    lane = lax.broadcasted_iota(jnp.int32, (chunk, LANES), 1)
    span = cores * capacity
    per_tile = LANES // span
    for chip in range(chips):
        tile = chosen[:, chip // per_tile * LANES : (chip // per_tile + 1) * LANES]
        shift = (quarter - span * (chip % per_tile)) % LANES
        moved = tile if shift == 0 else pltpu.roll(tile, shift, 1)
        value = jnp.where(lane < quarter, fresh, jnp.where(lane < quarter + span, moved, 0.0))
        message[chip] = value.astype(bf16)


def finish_body(
    core, near, far, master, first_moment, second_moment, filled,
    new_weight, new_master, new_first, new_second, *, groups, step, root,
):
    quarter, capacity = new_weight.shape[0], master.shape[0]
    chips, _, _ = near.shape
    lines = chips // groups
    rows = []
    for group in range(groups):
        block = []
        for line in range(lines):
            ours = near[line * groups + group].astype(f32)
            others = far[line * groups + group].astype(f32)
            block.append(jnp.where(core[0] == 0, ours, others))
            block.append(jnp.where(core[0] == 0, others, ours))
        rows.append(jnp.concatenate(block, axis=0)[:step])
    rows = jnp.concatenate(rows, axis=0).astype(bf16)
    unit = lax.broadcasted_iota(jnp.int32, (LANES, LANES), 0) == lax.broadcasted_iota(
        jnp.int32, (LANES, LANES), 1
    )
    turned = dot(jnp.where(unit, 1.0, 0.0).astype(bf16), rows, 1, 1)
    new_weight[...] = turned[:quarter].astype(bf16)
    low = turned[quarter : quarter + capacity]
    high = turned[quarter + capacity : quarter + 2 * capacity]
    grads = jnp.where(core[0] == 0, low, high) / root
    fresh, first_new, second_new = adam(
        grads, master[...], first_moment[...], second_moment[...]
    )
    keep = filled[...] > 0.0
    new_master[...] = jnp.where(keep, fresh, master[...])
    new_first[...] = jnp.where(keep, first_new, first_moment[...])
    new_second[...] = jnp.where(keep, second_new, second_moment[...])


def slot_tables(owner_list, capacity):
    count = owner_list.shape[0]
    same_owner = owner_list[:, None] == owner_list[None, :]
    order = jnp.arange(count, dtype=jnp.int32)
    earlier = order[None, :] < order[:, None]
    return owner_list * capacity + jnp.sum((same_owner & earlier).astype(jnp.int32), axis=1)


def exchange(value, axes):
    return lax.all_to_all(value, axes, 0, 0, tiled=True)


def local(latents, cotangent, weight, master, first_moment, second_moment, owner_list):
    lines, groups, cores, strips = (lax.axis_size(a) for a in ("line", "group", "core", "strip"))
    parts, chips = lines * cores, lines * groups
    ranks = parts * groups
    strip, core = lax.axis_index("strip"), lax.axis_index("core")
    rank = (lax.axis_index("line") * groups + lax.axis_index("group")) * cores + core
    strip_scalar = strip.reshape(1).astype(jnp.int32)
    channels, width = latents.shape[2:]
    quarter = channels // strips
    capacity = master.shape[0]
    share = TERMS * 3 * capacity // strips
    height = -(-share // 8) * 8
    taken = len(taps) * channels
    step = taken // groups
    padded = -(-step // LANES) * LANES
    chunk = padded // parts
    rows = strips
    root = float(ranks * rows * width) ** 0.5
    pixels, upstream = latents[0, 0], cotangent[0, 0]

    outgoing = pl.pallas_call(
        pack_body,
        out_shape=jax.ShapeDtypeStruct((strips, channels + quarter, width), bf16),
        in_specs=[pl.BlockSpec(memory_space=pl.ANY)] * 2,
        out_specs=pl.BlockSpec(memory_space=pl.ANY),
        scratch_shapes=[pltpu.SemaphoreType.DMA((2 * strips,))],
        name="pack",
        interpret=interpret,
    )(pixels, upstream.reshape(strips, quarter, width))
    gathered = exchange(outgoing, "strip")

    slot_ids = slot_tables(owner_list, capacity)
    slots = jnp.pad(
        slot_ids.reshape(strips, quarter), ((0, 0), (0, LANES - quarter)), constant_values=-1
    )
    owned = jnp.sum((owner_list == rank).astype(jnp.int32))
    filled = (jnp.arange(capacity, dtype=jnp.int32) < owned).astype(f32)[:, None]
    turned = weight.reshape(quarter, len(taps), channels).transpose(2, 1, 0)
    turned = turned.reshape(channels, len(taps) * quarter)
    pieces = call(
        functools.partial(split_body, strips=strips, step=step),
        jax.ShapeDtypeStruct((groups, height, padded), bf16),
        scalars=1,
        inputs=3,
    )(strip_scalar, master, first_moment, second_moment)
    gathered, slots, filled, turned, pieces = lax.optimization_barrier(
        (gathered, slots, filled, turned, pieces)
    )

    grads = call(
        functools.partial(gradient_body, channels=channels, step=step),
        jax.ShapeDtypeStruct((groups, quarter + height, padded), bf16),
        [pltpu.VMEM(((groups - 1) * step + padded, rows * width), bf16)],
    )(gathered, pieces)
    by_group = exchange(grads, "group")

    residual = lax.dynamic_slice_in_dim(gathered, strip * quarter, quarter, axis=1)
    results = call(
        functools.partial(convolution_body, channels=channels),
        [jax.ShapeDtypeStruct((quarter + channels, width), bf16)] * strips,
        [
            pltpu.VMEM((taken, rows * width), bf16),
            pltpu.VMEM((len(taps) * quarter, rows * width), bf16),
            pltpu.VMEM((rows, quarter + channels, width), bf16),
        ],
        scalars=1,
        inputs=4,
    )(strip_scalar, gathered, residual, weight, turned)

    returned = [
        lax.ppermute(result, "strip", [(i, (i + ahead) % strips) for i in range(strips)])
        if ahead
        else result
        for ahead, result in enumerate(results)
    ]

    by_part = call(
        functools.partial(turn_body, quarter=quarter, share=share),
        jax.ShapeDtypeStruct((parts, strips, chunk, LANES), bf16),
    )(by_group)
    by_part = exchange(
        by_part.reshape(parts * strips, chunk, LANES), ("line", "core", "strip")
    )
    message = call(
        functools.partial(
            publish_body, quarter=quarter, capacity=capacity, share=share, groups=groups,
            cores=cores, root=root,
        ),
        jax.ShapeDtypeStruct((chips, chunk, LANES), bf16),
        scalars=1,
        inputs=2,
    )(strip_scalar, by_part, slots)
    near = exchange(message, ("line", "group"))

    near, *returned = lax.optimization_barrier((near, *returned))
    output, grad_input = call(
        functools.partial(collect_body, quarter=quarter),
        [jax.ShapeDtypeStruct((channels, width), bf16)] * 2,
        scalars=1,
        inputs=2 + strips,
    )(strip_scalar, pixels, upstream, *returned)

    far = lax.ppermute(near, "core", [(i, cores - 1 - i) for i in range(cores)])
    new_weight, new_master, new_first, new_second = call(
        functools.partial(finish_body, groups=groups, step=step, root=root),
        [jax.ShapeDtypeStruct((quarter, taken), bf16)]
        + [jax.ShapeDtypeStruct(master.shape, f32)] * 3,
        scalars=1,
        inputs=6,
    )(core.reshape(1).astype(jnp.int32), near, far, master, first_moment, second_moment, filled)
    return (output[None, None], grad_input[None, None], new_weight, new_master, new_first, new_second)


def solution(mesh):
    fine = Mesh(
        mesh.devices.reshape(RANK_SHAPE + (mesh.shape["strip"],)),
        ("line", "group", "core", "strip"),
    )
    ranks = ("line", "group", "core")
    images = P(ranks, "strip", None, None)
    specs = (images, images, P("strip", None), P(ranks, None), P(ranks, None), P(ranks, None))

    return jax.shard_map(
        local, mesh=fine, in_specs=specs + (P(),), out_specs=specs, check_vma=False
    )
```

```python
import functools
import jax
import jax.numpy as jnp
from jax import lax
from jax.experimental import pallas as pl
from jax.experimental.pallas import tpu as pltpu
from jax.sharding import Mesh, PartitionSpec as P

beta_first = 0.9
beta_second = 0.999
learn_rate = 0.01
epsilon = 1e-08
bias_first = 1.0 - 0.9**10
bias_second = 1.0 - 0.999**10

interpret = False
LANES = 128
RANK_SHAPE = (8, 8, 2)
TERMS = 2
taps = [(dh, dw) for dh in (-1, 0, 1) for dw in (-1, 0, 1)]
f32 = jnp.float32
bf16 = jnp.bfloat16


def call(body, out_shape, scratch=(), scalars=0, inputs=0):
    specs = {}
    if scalars:
        specs["in_specs"] = [pl.BlockSpec(memory_space=pltpu.SMEM)] * scalars + [
            pl.BlockSpec(memory_space=pltpu.VMEM)
        ] * inputs
    return pl.pallas_call(
        body,
        out_shape=out_shape,
        scratch_shapes=scratch,
        interpret=interpret,
        compiler_params=pltpu.CompilerParams(vmem_limit_bytes=20 << 20),
        **specs,
    )


def dot(left, right, left_dim, right_dim):
    return lax.dot_general(
        left, right, (((left_dim,), (right_dim,)), ((), ())), preferred_element_type=f32
    )


def shifted(value):
    lane = lax.broadcasted_iota(jnp.int32, value.shape, 1)
    last = value.shape[1] - 1
    before = jnp.where(lane == 0, 0.0, pltpu.roll(value, 1, 1))
    after = jnp.where(lane == last, 0.0, pltpu.roll(value, last, 1))
    return {-1: before.astype(bf16), 0: value.astype(bf16), 1: after.astype(bf16)}


def fill(cols, rows, load, direction):
    first = load(0)
    count, width = first.shape
    for index, (dh, _) in enumerate(taps):
        for h in range(rows):
            if not 0 <= h + direction * dh < rows:
                cols[index * count : (index + 1) * count, h * width : (h + 1) * width] = jnp.zeros(
                    (count, width), bf16
                )
    for source in range(rows):
        versions = shifted(first if source == 0 else load(source))
        for index, (dh, dw) in enumerate(taps):
            h = source - direction * dh
            if 0 <= h < rows:
                cols[index * count : (index + 1) * count, h * width : (h + 1) * width] = versions[
                    direction * dw
                ]


def activated(gathered, channels, h):
    value = gathered[h, :channels, :].astype(f32)
    return (value / (1.0 + jnp.exp(-value))).astype(bf16).astype(f32)


def pack_body(pixels, upstream, outgoing, staged, arrived):
    strips, channels = outgoing.shape[0], pixels.shape[0]
    loads = [
        pltpu.make_async_copy(pixels, staged.at[:channels, :], arrived.at[0]),
        pltpu.make_async_copy(upstream, staged.at[channels:, :], arrived.at[1]),
    ]
    for load in loads:
        load.start()
    for load in loads:
        load.wait()
    quarter = channels // strips
    for strip in range(strips):
        outgoing[strip, :channels, :] = staged[:channels, :]
        outgoing[strip, channels:, :] = staged[
            channels + strip * quarter : channels + (strip + 1) * quarter, :
        ]


def split_body(master, first_moment, second_moment, pieces, *, step):
    state = jnp.concatenate([master[...], first_moment[...], second_moment[...]], axis=0)
    terms = []
    for _ in range(TERMS):
        term = state.astype(bf16).astype(f32)
        terms.append(term)
        state = state - term
    terms = jnp.concatenate(terms, axis=0)
    halves, height, padded = pieces.shape
    excess = (halves - 1) * step + padded - terms.shape[1]
    terms = jnp.concatenate([terms, jnp.zeros((height, excess), f32)], axis=1)
    for half in range(halves):
        pieces[half] = terms[:, half * step : half * step + padded].astype(bf16)


def gradient_body(core, gathered, pieces, kept, sent, cols, *, channels, step):
    rows = gathered.shape[0]
    quarter = gathered.shape[1] - channels
    fill(cols, rows, functools.partial(activated, gathered, channels), 1)
    whole = len(taps) * channels
    if cols.shape[0] > whole:
        cols[whole:, :] = jnp.zeros((cols.shape[0] - whole, cols.shape[1]), bf16)
    upstream = jnp.concatenate([gathered[h, channels:, :] for h in range(rows)], axis=1)
    padded = kept.shape[1]
    for target, half in ((sent, 1 - core[0]), (kept, core[0])):
        start = pl.multiple_of(half * step, 8)
        product = dot(upstream, cols[pl.ds(start, padded), :], 1, 1)
        target[:quarter, :] = product.astype(bf16)
        target[quarter:, :] = pieces[half]


def convolution_body(
    strip, gathered, residual, weight, turned, *results, channels
):
    *results, cols, back_cols, whole = results
    rows, quarter, width = residual.shape
    fill(cols, rows, functools.partial(activated, gathered, channels), 1)
    convolved = dot(weight[...], cols[...], 1, 0)
    for h in range(rows):
        whole[h, :quarter, :] = (
            residual[h].astype(f32) + convolved[:, h * width : (h + 1) * width]
        ).astype(bf16)
    fill(back_cols, rows, lambda h: gathered[h, channels:, :].astype(f32), -1)
    spread = dot(turned[...], back_cols[...], 1, 0)
    for h in range(rows):
        whole[h, quarter:, :] = spread[:, h * width : (h + 1) * width].astype(bf16)
    for ahead, result in enumerate(results):
        target = strip[0] + ahead
        result[...] = whole[jnp.where(target >= rows, target - rows, target)]


def collect_body(strip, pixels, upstream, *pieces, quarter):
    *pieces, output, grad_input = pieces
    strips = len(pieces)
    spread = jnp.zeros(pixels.shape, f32)
    for behind, piece in enumerate(pieces):
        source = strip[0] - behind
        source = jnp.where(source < 0, source + strips, source)
        output[pl.ds(pl.multiple_of(source * quarter, quarter), quarter), :] = piece[:quarter, :]
        spread = spread + piece[quarter:, :].astype(f32)
    value = pixels[...].astype(f32)
    sigmoid = 1.0 / (1.0 + jnp.exp(-value))
    derivative = sigmoid * (1.0 + value * (1.0 - sigmoid))
    grad_input[...] = (upstream[...].astype(f32) + spread * derivative).astype(bf16)


def turn_body(core, kept, received, message, *, quarter):
    ours, others = kept[...].astype(f32), received[...].astype(f32)
    first = core[0] == 0
    rows = [
        ours[:quarter] + others[:quarter],
        jnp.where(first, ours[quarter:], others[quarter:]),
        jnp.where(first, others[quarter:], ours[quarter:]),
    ]
    spare = LANES - 2 * ours.shape[0] + quarter
    if spare:
        rows.append(jnp.zeros((spare, ours.shape[1]), f32))
    turned = jnp.transpose(jnp.concatenate(rows, axis=0))
    chips, chunk, _ = message.shape
    for chip in range(chips):
        message[chip] = turned[chip * chunk : (chip + 1) * chunk, :].astype(bf16)


def adam(grads, master, first_moment, second_moment):
    first_new = beta_first * first_moment + (1.0 - beta_first) * grads
    second_new = beta_second * second_moment + (1.0 - beta_second) * grads * grads
    update = learn_rate * (first_new / bias_first) / (jnp.sqrt(second_new / bias_second) + epsilon)
    return master - update, first_new, second_new


def publish_body(strip, received, slots, message, *, quarter, capacity, cores, root):
    chips, chunk, _ = received.shape
    strips = slots.shape[0]
    columns = max(LANES, chips * cores * capacity)
    mine = slots[0:1, :]
    for other in range(1, strips):
        mine = jnp.where(strip[0] == other, slots[other : other + 1, :], mine)
    wide = jnp.concatenate([mine] * 3, axis=1)
    owner, place = wide // capacity, wide % capacity
    share = TERMS * 3 * capacity
    row = lax.broadcasted_iota(jnp.int32, (LANES, 3 * LANES), 0) - quarter
    array = lax.broadcasted_iota(jnp.int32, (LANES, 3 * LANES), 1) // LANES
    within = row % (3 * capacity)
    here = (row >= 0) & (row < cores * share) & (wide >= 0) & (row // share == owner % cores)
    here = here & (within // capacity == array) & (within % capacity == place)
    here = jnp.where(here, 1.0, 0.0).astype(bf16)
    values = [received[chip].astype(f32) for chip in range(chips)]
    grads = values[0]
    for value in values[1:]:
        grads = grads + value
    picked = dot(jnp.concatenate(values, axis=0).astype(bf16), here, 1, 0)
    state = jnp.zeros((chunk, 3 * LANES), f32)
    for chip in range(chips):
        state = jnp.where(
            owner // cores == chip, picked[chip * chunk : (chip + 1) * chunk], state
        )
    fresh, _, _ = adam(
        grads / root, state[:, :LANES], state[:, LANES : 2 * LANES], state[:, 2 * LANES :]
    )
    index = lax.broadcasted_iota(jnp.int32, (columns, LANES), 0)
    matches = jnp.where(index == mine, 1.0, 0.0).astype(bf16)
    chosen = dot(grads.astype(bf16), matches, 1, 1)
    lane = lax.broadcasted_iota(jnp.int32, (chunk, LANES), 1)
    span = cores * capacity
    per_tile = LANES // span
    for chip in range(chips):
        tile = chosen[:, chip // per_tile * LANES : (chip // per_tile + 1) * LANES]
        shift = (quarter - span * (chip % per_tile)) % LANES
        moved = tile if shift == 0 else pltpu.roll(tile, shift, 1)
        value = jnp.where(lane < quarter, fresh, jnp.where(lane < quarter + span, moved, 0.0))
        message[chip] = value.astype(bf16)


def flat(messages):
    chips, chunk, _ = messages.shape
    return messages[...].astype(f32).reshape(chips * chunk, LANES)


def unit(rows, first):
    shape = (rows, LANES)
    row = lax.broadcasted_iota(jnp.int32, shape, 0)
    return jnp.where(row + first == lax.broadcasted_iota(jnp.int32, shape, 1), 1.0, 0.0).astype(
        bf16
    )


def owned_body(near, message, *, quarter, capacity, strips):
    targets, height, _ = message.shape
    turned = dot(unit(16, quarter), flat(near).astype(bf16), 1, 1)
    for target in range(targets):
        first = target // strips * capacity
        rows = turned[first : first + capacity]
        rows = jnp.concatenate([rows, jnp.zeros((height - capacity, rows.shape[1]), f32)], axis=0)
        message[target] = rows.astype(bf16)


def finish_body(
    core, near, far, owned, master, first_moment, second_moment, filled,
    new_weight, new_master, new_first, new_second, *, step, strips, root,
):
    quarter, capacity = new_weight.shape[0], master.shape[0]
    ours, others = flat(near), flat(far)
    first = core[0] == 0
    rows = [jnp.where(first, ours, others)[:step], jnp.where(first, others, ours)[:step]]
    rows = jnp.concatenate(rows, axis=0).astype(bf16)
    turned = dot(unit(quarter, 0), rows, 1, 1)
    new_weight[...] = turned.astype(bf16)
    halves = []
    for half in range(owned.shape[0] // strips):
        total = owned[half * strips].astype(f32)
        for strip in range(1, strips):
            total = total + owned[half * strips + strip].astype(f32)
        halves.append(total[:capacity, :step])
    grads = jnp.concatenate(halves, axis=1) / root
    fresh, first_new, second_new = adam(
        grads, master[...], first_moment[...], second_moment[...]
    )
    keep = filled[...] > 0.0
    new_master[...] = jnp.where(keep, fresh, master[...])
    new_first[...] = jnp.where(keep, first_new, first_moment[...])
    new_second[...] = jnp.where(keep, second_new, second_moment[...])


def slot_tables(owner_list, capacity):
    count = owner_list.shape[0]
    same_owner = owner_list[:, None] == owner_list[None, :]
    order = jnp.arange(count, dtype=jnp.int32)
    earlier = order[None, :] < order[:, None]
    return owner_list * capacity + jnp.sum((same_owner & earlier).astype(jnp.int32), axis=1)


def exchange(value, axes):
    return lax.all_to_all(value, axes, 0, 0, tiled=True)


def local(latents, cotangent, weight, master, first_moment, second_moment, owner_list):
    lines, groups, cores, strips = (lax.axis_size(a) for a in ("line", "group", "core", "strip"))
    chips = lines * groups
    ranks = chips * cores
    strip, core = lax.axis_index("strip"), lax.axis_index("core")
    rank = (lax.axis_index("line") * groups + lax.axis_index("group")) * cores + core
    strip_scalar = strip.reshape(1).astype(jnp.int32)
    core_scalar = core.reshape(1).astype(jnp.int32)
    swap = [(i, cores - 1 - i) for i in range(cores)]
    channels, width = latents.shape[2:]
    quarter = channels // strips
    capacity = master.shape[0]
    height = TERMS * 3 * capacity
    taken = len(taps) * channels
    step = taken // cores
    padded = -(-step // LANES) * LANES
    chunk = padded // chips
    rows = strips
    root = float(ranks * rows * width) ** 0.5
    pixels, upstream = latents[0, 0], cotangent[0, 0]

    outgoing = pl.pallas_call(
        pack_body,
        out_shape=jax.ShapeDtypeStruct((strips, channels + quarter, width), bf16),
        in_specs=[pl.BlockSpec(memory_space=pltpu.HBM)] * 2,
        scratch_shapes=[
            pltpu.VMEM((2 * channels, width), bf16),
            pltpu.SemaphoreType.DMA((2,)),
        ],
        name="pack",
        interpret=interpret,
        compiler_params=pltpu.CompilerParams(vmem_limit_bytes=4 << 20),
    )(pixels, upstream)
    gathered = exchange(outgoing, "strip")

    slot_ids = slot_tables(owner_list, capacity)
    slots = jnp.pad(
        slot_ids.reshape(strips, quarter), ((0, 0), (0, LANES - quarter)), constant_values=-1
    )
    owned = jnp.sum((owner_list == rank).astype(jnp.int32))
    filled = (jnp.arange(capacity, dtype=jnp.int32) < owned).astype(f32)[:, None]
    turned = weight.reshape(quarter, len(taps), channels).transpose(2, 1, 0)
    turned = turned.reshape(channels, len(taps) * quarter)
    pieces = call(
        functools.partial(split_body, step=step),
        jax.ShapeDtypeStruct((cores, height, padded), bf16),
    )(master, first_moment, second_moment)
    gathered, slots, filled, turned, pieces = lax.optimization_barrier(
        (gathered, slots, filled, turned, pieces)
    )

    kept, sent = call(
        functools.partial(gradient_body, channels=channels, step=step),
        [jax.ShapeDtypeStruct((quarter + height, padded), bf16)] * 2,
        [pltpu.VMEM(((cores - 1) * step + padded, rows * width), bf16)],
        scalars=1,
        inputs=2,
    )(core_scalar, gathered, pieces)
    swapped = lax.ppermute(sent, "core", swap)

    residual = lax.dynamic_slice_in_dim(gathered, strip * quarter, quarter, axis=1)
    results = call(
        functools.partial(convolution_body, channels=channels),
        [jax.ShapeDtypeStruct((quarter + channels, width), bf16)] * strips,
        [
            pltpu.VMEM((taken, rows * width), bf16),
            pltpu.VMEM((len(taps) * quarter, rows * width), bf16),
            pltpu.VMEM((rows, quarter + channels, width), bf16),
        ],
        scalars=1,
        inputs=4,
    )(strip_scalar, gathered, residual, weight, turned)

    returned = [
        lax.ppermute(result, "strip", [(i, (i + ahead) % strips) for i in range(strips)])
        if ahead
        else result
        for ahead, result in enumerate(results)
    ]

    by_chip = call(
        functools.partial(turn_body, quarter=quarter),
        jax.ShapeDtypeStruct((chips, chunk, LANES), bf16),
        scalars=1,
        inputs=2,
    )(core_scalar, kept, swapped)
    by_chip = exchange(by_chip, ("line", "group"))
    message = call(
        functools.partial(publish_body, quarter=quarter, capacity=capacity, cores=cores, root=root),
        jax.ShapeDtypeStruct((chips, chunk, LANES), bf16),
        scalars=1,
        inputs=2,
    )(strip_scalar, by_chip, slots)
    near = exchange(message, ("line", "group"))

    near, *returned = lax.optimization_barrier((near, *returned))
    output, grad_input = call(
        functools.partial(collect_body, quarter=quarter),
        [jax.ShapeDtypeStruct((channels, width), bf16)] * 2,
        scalars=1,
        inputs=2 + strips,
    )(strip_scalar, pixels, upstream, *returned)

    far = lax.ppermute(near, "core", swap)
    owned_rows = call(
        functools.partial(owned_body, quarter=quarter, capacity=capacity, strips=strips),
        jax.ShapeDtypeStruct((cores * strips, 8, padded), bf16),
    )(near)
    owned_rows = exchange(owned_rows, ("core", "strip"))
    new_weight, new_master, new_first, new_second = call(
        functools.partial(finish_body, step=step, strips=strips, root=root),
        [jax.ShapeDtypeStruct((quarter, taken), bf16)]
        + [jax.ShapeDtypeStruct(master.shape, f32)] * 3,
        scalars=1,
        inputs=7,
    )(core_scalar, near, far, owned_rows, master, first_moment, second_moment, filled)
    return (output[None, None], grad_input[None, None], new_weight, new_master, new_first, new_second)


def solution(mesh):
    fine = Mesh(
        mesh.devices.reshape(RANK_SHAPE + (mesh.shape["strip"],)),
        ("line", "group", "core", "strip"),
    )
    ranks = ("line", "group", "core")
    images = P(ranks, "strip", None, None)
    specs = (images, images, P("strip", None), P(ranks, None), P(ranks, None), P(ranks, None))

    return jax.shard_map(
        local, mesh=fine, in_specs=specs + (P(),), out_specs=specs, check_vma=False
    )
```

```python
import functools
import jax
import jax.numpy as jnp
from jax import lax
from jax.experimental import pallas as pl
from jax.experimental.pallas import tpu as pltpu
from jax.sharding import Mesh, PartitionSpec as P

beta_first = 0.9
beta_second = 0.999
learn_rate = 0.01
epsilon = 1e-08
bias_first = 1.0 - 0.9**10
bias_second = 1.0 - 0.999**10

interpret = False
LANES = 128
RANK_SHAPE = (8, 8, 2)
TERMS = 2
taps = [(dh, dw) for dh in (-1, 0, 1) for dw in (-1, 0, 1)]
f32 = jnp.float32
bf16 = jnp.bfloat16


def call(body, out_shape, scratch=(), scalars=0, inputs=0):
    specs = {}
    if scalars:
        specs["in_specs"] = [pl.BlockSpec(memory_space=pltpu.SMEM)] * scalars + [
            pl.BlockSpec(memory_space=pltpu.VMEM)
        ] * inputs
    return pl.pallas_call(
        body,
        out_shape=out_shape,
        scratch_shapes=scratch,
        interpret=interpret,
        compiler_params=pltpu.CompilerParams(vmem_limit_bytes=20 << 20),
        **specs,
    )


def dot(left, right, left_dim, right_dim):
    return lax.dot_general(
        left, right, (((left_dim,), (right_dim,)), ((), ())), preferred_element_type=f32
    )


def shifted(value):
    lane = lax.broadcasted_iota(jnp.int32, value.shape, 1)
    last = value.shape[1] - 1
    before = jnp.where(lane == 0, 0.0, pltpu.roll(value, 1, 1))
    after = jnp.where(lane == last, 0.0, pltpu.roll(value, last, 1))
    return {-1: before.astype(bf16), 0: value.astype(bf16), 1: after.astype(bf16)}


def fill(cols, rows, load, direction):
    first = load(0)
    count, width = first.shape
    for index, (dh, _) in enumerate(taps):
        for h in range(rows):
            if not 0 <= h + direction * dh < rows:
                cols[index * count : (index + 1) * count, h * width : (h + 1) * width] = jnp.zeros(
                    (count, width), bf16
                )
    for source in range(rows):
        versions = shifted(first if source == 0 else load(source))
        for index, (dh, dw) in enumerate(taps):
            h = source - direction * dh
            if 0 <= h < rows:
                cols[index * count : (index + 1) * count, h * width : (h + 1) * width] = versions[
                    direction * dw
                ]


def activated(gathered, channels, h):
    value = gathered[h, :channels, :].astype(f32)
    return (value / (1.0 + jnp.exp(-value))).astype(bf16).astype(f32)


def pack_body(pixels, upstream, outgoing, staged, arrived):
    strips, channels = outgoing.shape[0], pixels.shape[0]
    loads = [
        pltpu.make_async_copy(pixels, staged.at[:channels, :], arrived.at[0]),
        pltpu.make_async_copy(upstream, staged.at[channels:, :], arrived.at[1]),
    ]
    for load in loads:
        load.start()
    for load in loads:
        load.wait()
    quarter = channels // strips
    for strip in range(strips):
        outgoing[strip, :channels, :] = staged[:channels, :]
        outgoing[strip, channels:, :] = staged[
            channels + strip * quarter : channels + (strip + 1) * quarter, :
        ]


def split_body(master, first_moment, second_moment, pieces, *, step):
    state = jnp.concatenate([master[...], first_moment[...], second_moment[...]], axis=0)
    terms = []
    for _ in range(TERMS):
        term = state.astype(bf16).astype(f32)
        terms.append(term)
        state = state - term
    terms = jnp.concatenate(terms, axis=0)
    halves, height, padded = pieces.shape
    excess = (halves - 1) * step + padded - terms.shape[1]
    terms = jnp.concatenate([terms, jnp.zeros((height, excess), f32)], axis=1)
    for half in range(halves):
        pieces[half] = terms[:, half * step : half * step + padded].astype(bf16)


def gradient_body(core, gathered, pieces, kept, sent, cols, *, channels, step):
    rows = gathered.shape[0]
    quarter = gathered.shape[1] - channels
    fill(cols, rows, functools.partial(activated, gathered, channels), 1)
    whole = len(taps) * channels
    if cols.shape[0] > whole:
        cols[whole:, :] = jnp.zeros((cols.shape[0] - whole, cols.shape[1]), bf16)
    upstream = jnp.concatenate([gathered[h, channels:, :] for h in range(rows)], axis=1)
    padded = kept.shape[1]
    for target, half in ((sent, 1 - core[0]), (kept, core[0])):
        start = pl.multiple_of(half * step, 8)
        product = dot(upstream, cols[pl.ds(start, padded), :], 1, 1)
        target[:quarter, :] = product.astype(bf16)
        target[quarter:, :] = pieces[half]


def convolution_body(
    strip, gathered, residual, weight, turned, *results, channels
):
    *results, cols, back_cols, whole = results
    rows, quarter, width = residual.shape
    fill(cols, rows, functools.partial(activated, gathered, channels), 1)
    convolved = dot(weight[...], cols[...], 1, 0)
    for h in range(rows):
        whole[h, :quarter, :] = (
            residual[h].astype(f32) + convolved[:, h * width : (h + 1) * width]
        ).astype(bf16)
    fill(back_cols, rows, lambda h: gathered[h, channels:, :].astype(f32), -1)
    spread = dot(turned[...], back_cols[...], 1, 0)
    for h in range(rows):
        whole[h, quarter:, :] = spread[:, h * width : (h + 1) * width].astype(bf16)
    for ahead, result in enumerate(results):
        target = strip[0] + ahead
        result[...] = whole[jnp.where(target >= rows, target - rows, target)]


def collect_body(strip, pixels, upstream, *pieces, quarter):
    *pieces, output, grad_input = pieces
    strips = len(pieces)
    spread = jnp.zeros(pixels.shape, f32)
    for behind, piece in enumerate(pieces):
        source = strip[0] - behind
        source = jnp.where(source < 0, source + strips, source)
        output[pl.ds(pl.multiple_of(source * quarter, quarter), quarter), :] = piece[:quarter, :]
        spread = spread + piece[quarter:, :].astype(f32)
    value = pixels[...].astype(f32)
    sigmoid = 1.0 / (1.0 + jnp.exp(-value))
    derivative = sigmoid * (1.0 + value * (1.0 - sigmoid))
    grad_input[...] = (upstream[...].astype(f32) + spread * derivative).astype(bf16)


def turn_body(core, kept, received, message, *, quarter):
    ours, others = kept[...].astype(f32), received[...].astype(f32)
    first = core[0] == 0
    rows = [
        ours[:quarter] + others[:quarter],
        jnp.where(first, ours[quarter:], others[quarter:]),
        jnp.where(first, others[quarter:], ours[quarter:]),
    ]
    spare = LANES - 2 * ours.shape[0] + quarter
    if spare:
        rows.append(jnp.zeros((spare, ours.shape[1]), f32))
    turned = jnp.transpose(jnp.concatenate(rows, axis=0))
    chips, chunk, _ = message.shape
    for chip in range(chips):
        message[chip] = turned[chip * chunk : (chip + 1) * chunk, :].astype(bf16)


def adam(grads, master, first_moment, second_moment):
    first_new = beta_first * first_moment + (1.0 - beta_first) * grads
    second_new = beta_second * second_moment + (1.0 - beta_second) * grads * grads
    update = learn_rate * (first_new / bias_first) / (jnp.sqrt(second_new / bias_second) + epsilon)
    return master - update, first_new, second_new


def publish_body(strip, received, slots, message, *, quarter, capacity, cores, root):
    chips, chunk, _ = received.shape
    strips = slots.shape[0]
    columns = max(LANES, chips * cores * capacity)
    mine = slots[0:1, :]
    for other in range(1, strips):
        mine = jnp.where(strip[0] == other, slots[other : other + 1, :], mine)
    wide = jnp.concatenate([mine] * 3, axis=1)
    owner, place = wide // capacity, wide % capacity
    share = TERMS * 3 * capacity
    row = lax.broadcasted_iota(jnp.int32, (LANES, 3 * LANES), 0) - quarter
    array = lax.broadcasted_iota(jnp.int32, (LANES, 3 * LANES), 1) // LANES
    within = row % (3 * capacity)
    here = (row >= 0) & (row < cores * share) & (wide >= 0) & (row // share == owner % cores)
    here = here & (within // capacity == array) & (within % capacity == place)
    here = jnp.where(here, 1.0, 0.0).astype(bf16)
    values = [received[chip].astype(f32) for chip in range(chips)]
    grads = values[0]
    for value in values[1:]:
        grads = grads + value
    picked = dot(jnp.concatenate(values, axis=0).astype(bf16), here, 1, 0)
    state = jnp.zeros((chunk, 3 * LANES), f32)
    for chip in range(chips):
        state = jnp.where(
            owner // cores == chip, picked[chip * chunk : (chip + 1) * chunk], state
        )
    fresh, _, _ = adam(
        grads / root, state[:, :LANES], state[:, LANES : 2 * LANES], state[:, 2 * LANES :]
    )
    index = lax.broadcasted_iota(jnp.int32, (columns, LANES), 0)
    matches = jnp.where(index == mine, 1.0, 0.0).astype(bf16)
    chosen = dot(grads.astype(bf16), matches, 1, 1)
    lane = lax.broadcasted_iota(jnp.int32, (chunk, LANES), 1)
    span = cores * capacity
    per_tile = LANES // span
    for chip in range(chips):
        tile = chosen[:, chip // per_tile * LANES : (chip // per_tile + 1) * LANES]
        shift = (quarter - span * (chip % per_tile)) % LANES
        moved = tile if shift == 0 else pltpu.roll(tile, shift, 1)
        value = jnp.where(lane < quarter, fresh, jnp.where(lane < quarter + span, moved, 0.0))
        message[chip] = value.astype(bf16)


def flat(messages):
    chips, chunk, _ = messages.shape
    return messages[...].astype(f32).reshape(chips * chunk, LANES)


def unit(rows, first):
    shape = (rows, LANES)
    row = lax.broadcasted_iota(jnp.int32, shape, 0)
    return jnp.where(row + first == lax.broadcasted_iota(jnp.int32, shape, 1), 1.0, 0.0).astype(
        bf16
    )


def owned_body(near, message, *, quarter, capacity, strips):
    targets = message.shape[0]
    turned = dot(unit(16, quarter), flat(near).astype(bf16), 1, 1)
    for target in range(targets):
        first = target // strips * capacity
        message[target] = turned[first : first + capacity].astype(bf16)


def finish_body(
    core, near, far, owned, master, first_moment, second_moment, filled,
    new_weight, new_master, new_first, new_second, *, step, strips, root,
):
    quarter, capacity = new_weight.shape[0], master.shape[0]
    ours, others = flat(near), flat(far)
    first = core[0] == 0
    rows = [jnp.where(first, ours, others)[:step], jnp.where(first, others, ours)[:step]]
    rows = jnp.concatenate(rows, axis=0).astype(bf16)
    turned = dot(unit(quarter, 0), rows, 1, 1)
    new_weight[...] = turned.astype(bf16)
    halves = []
    for half in range(owned.shape[0] // strips):
        total = owned[half * strips].astype(f32)
        for strip in range(1, strips):
            total = total + owned[half * strips + strip].astype(f32)
        halves.append(total[:capacity, :step])
    grads = jnp.concatenate(halves, axis=1) / root
    fresh, first_new, second_new = adam(
        grads, master[...], first_moment[...], second_moment[...]
    )
    keep = filled[...] > 0.0
    new_master[...] = jnp.where(keep, fresh, master[...])
    new_first[...] = jnp.where(keep, first_new, first_moment[...])
    new_second[...] = jnp.where(keep, second_new, second_moment[...])


def slot_tables(owner_list, capacity):
    count = owner_list.shape[0]
    same_owner = owner_list[:, None] == owner_list[None, :]
    order = jnp.arange(count, dtype=jnp.int32)
    earlier = order[None, :] < order[:, None]
    return owner_list * capacity + jnp.sum((same_owner & earlier).astype(jnp.int32), axis=1)


def exchange(value, axes):
    return lax.all_to_all(value, axes, 0, 0, tiled=True)


def local(latents, cotangent, weight, master, first_moment, second_moment, owner_list):
    lines, groups, cores, strips = (lax.axis_size(a) for a in ("line", "group", "core", "strip"))
    chips = lines * groups
    ranks = chips * cores
    strip, core = lax.axis_index("strip"), lax.axis_index("core")
    rank = (lax.axis_index("line") * groups + lax.axis_index("group")) * cores + core
    strip_scalar = strip.reshape(1).astype(jnp.int32)
    core_scalar = core.reshape(1).astype(jnp.int32)
    swap = [(i, cores - 1 - i) for i in range(cores)]
    channels, width = latents.shape[2:]
    quarter = channels // strips
    capacity = master.shape[0]
    height = TERMS * 3 * capacity
    taken = len(taps) * channels
    step = taken // cores
    padded = -(-step // LANES) * LANES
    chunk = padded // chips
    rows = strips
    root = float(ranks * rows * width) ** 0.5
    pixels, upstream = latents[0, 0], cotangent[0, 0]

    outgoing = pl.pallas_call(
        pack_body,
        out_shape=jax.ShapeDtypeStruct((strips, channels + quarter, width), bf16),
        in_specs=[pl.BlockSpec(memory_space=pltpu.HBM)] * 2,
        scratch_shapes=[
            pltpu.VMEM((2 * channels, width), bf16),
            pltpu.SemaphoreType.DMA((2,)),
        ],
        name="pack",
        interpret=interpret,
        compiler_params=pltpu.CompilerParams(vmem_limit_bytes=60 << 20),
    )(pixels, upstream)
    gathered = exchange(outgoing, "strip")

    slot_ids = slot_tables(owner_list, capacity)
    slots = jnp.pad(
        slot_ids.reshape(strips, quarter), ((0, 0), (0, LANES - quarter)), constant_values=-1
    )
    owned = jnp.sum((owner_list == rank).astype(jnp.int32))
    filled = (jnp.arange(capacity, dtype=jnp.int32) < owned).astype(f32)[:, None]
    turned = weight.reshape(quarter, len(taps), channels).transpose(2, 1, 0)
    turned = turned.reshape(channels, len(taps) * quarter)
    pieces = call(
        functools.partial(split_body, step=step),
        jax.ShapeDtypeStruct((cores, height, padded), bf16),
    )(master, first_moment, second_moment)
    gathered, slots, filled, turned, pieces = lax.optimization_barrier(
        (gathered, slots, filled, turned, pieces)
    )

    kept, sent = call(
        functools.partial(gradient_body, channels=channels, step=step),
        [jax.ShapeDtypeStruct((quarter + height, padded), bf16)] * 2,
        [pltpu.VMEM(((cores - 1) * step + padded, rows * width), bf16)],
        scalars=1,
        inputs=2,
    )(core_scalar, gathered, pieces)
    swapped = lax.ppermute(sent, "core", swap)

    residual = lax.dynamic_slice_in_dim(gathered, strip * quarter, quarter, axis=1)
    results = call(
        functools.partial(convolution_body, channels=channels),
        [jax.ShapeDtypeStruct((quarter + channels, width), bf16)] * strips,
        [
            pltpu.VMEM((taken, rows * width), bf16),
            pltpu.VMEM((len(taps) * quarter, rows * width), bf16),
            pltpu.VMEM((rows, quarter + channels, width), bf16),
        ],
        scalars=1,
        inputs=4,
    )(strip_scalar, gathered, residual, weight, turned)

    returned = [results[0]]
    for ahead in range(1, strips):
        pairs = [(i, (i + ahead) % strips) for i in range(strips)]
        returned.append(lax.ppermute(results[ahead], "strip", pairs))

    by_chip = call(
        functools.partial(turn_body, quarter=quarter),
        jax.ShapeDtypeStruct((chips, chunk, LANES), bf16),
        scalars=1,
        inputs=2,
    )(core_scalar, kept, swapped)
    by_chip = exchange(by_chip, ("line", "group"))
    message = call(
        functools.partial(publish_body, quarter=quarter, capacity=capacity, cores=cores, root=root),
        jax.ShapeDtypeStruct((chips, chunk, LANES), bf16),
        scalars=1,
        inputs=2,
    )(strip_scalar, by_chip, slots)
    near = exchange(message, ("line", "group"))

    output, grad_input = call(
        functools.partial(collect_body, quarter=quarter),
        [jax.ShapeDtypeStruct((channels, width), bf16)] * 2,
        scalars=1,
        inputs=2 + strips,
    )(strip_scalar, pixels, upstream, *returned)

    far = lax.ppermute(near, "core", swap)
    owned_rows = call(
        functools.partial(owned_body, quarter=quarter, capacity=capacity, strips=strips),
        jax.ShapeDtypeStruct((cores * strips, capacity, padded), bf16),
    )(near)
    owned_rows = exchange(owned_rows, ("core", "strip"))
    new_weight, new_master, new_first, new_second = call(
        functools.partial(finish_body, step=step, strips=strips, root=root),
        [jax.ShapeDtypeStruct((quarter, taken), bf16)]
        + [jax.ShapeDtypeStruct(master.shape, f32)] * 3,
        scalars=1,
        inputs=7,
    )(core_scalar, near, far, owned_rows, master, first_moment, second_moment, filled)
    return (output[None, None], grad_input[None, None], new_weight, new_master, new_first, new_second)


def solution(mesh):
    fine = Mesh(
        mesh.devices.reshape(RANK_SHAPE + (mesh.shape["strip"],)),
        ("line", "group", "core", "strip"),
    )
    ranks = ("line", "group", "core")
    images = P(ranks, "strip", None, None)
    specs = (images, images, P("strip", None), P(ranks, None), P(ranks, None), P(ranks, None))

    return jax.shard_map(
        local, mesh=fine, in_specs=specs + (P(),), out_specs=specs, check_vma=False
    )
```

```python
import functools
import jax
import jax.numpy as jnp
from jax import lax
from jax.experimental import pallas as pl
from jax.experimental.pallas import tpu as pltpu
from jax.sharding import Mesh, PartitionSpec as P

beta_first = 0.9
beta_second = 0.999
learn_rate = 0.01
epsilon = 1e-08
bias_first = 1.0 - 0.9**10
bias_second = 1.0 - 0.999**10

interpret = False
LANES = 128
RANK_SHAPE = (8, 4, 2, 2)
TERMS = 2
taps = [(dh, dw) for dh in (-1, 0, 1) for dw in (-1, 0, 1)]
f32 = jnp.float32
bf16 = jnp.bfloat16


def call(body, out_shape, scratch=(), scalars=0, inputs=0):
    specs = {}
    if scalars:
        specs["in_specs"] = [pl.BlockSpec(memory_space=pltpu.SMEM)] * scalars + [
            pl.BlockSpec(memory_space=pltpu.VMEM)
        ] * inputs
    return pl.pallas_call(
        body,
        out_shape=out_shape,
        scratch_shapes=scratch,
        interpret=interpret,
        compiler_params=pltpu.CompilerParams(vmem_limit_bytes=20 << 20),
        **specs,
    )


def dot(left, right, left_dim, right_dim):
    return lax.dot_general(
        left, right, (((left_dim,), (right_dim,)), ((), ())), preferred_element_type=f32
    )


def shifted(value):
    lane = lax.broadcasted_iota(jnp.int32, value.shape, 1)
    last = value.shape[1] - 1
    before = jnp.where(lane == 0, 0.0, pltpu.roll(value, 1, 1))
    after = jnp.where(lane == last, 0.0, pltpu.roll(value, last, 1))
    return {-1: before.astype(bf16), 0: value.astype(bf16), 1: after.astype(bf16)}


def fill(cols, rows, load, direction):
    first = load(0)
    count, width = first.shape
    for index, (dh, _) in enumerate(taps):
        for h in range(rows):
            if not 0 <= h + direction * dh < rows:
                cols[index * count : (index + 1) * count, h * width : (h + 1) * width] = jnp.zeros(
                    (count, width), bf16
                )
    for source in range(rows):
        versions = shifted(first if source == 0 else load(source))
        for index, (dh, dw) in enumerate(taps):
            h = source - direction * dh
            if 0 <= h < rows:
                cols[index * count : (index + 1) * count, h * width : (h + 1) * width] = versions[
                    direction * dw
                ]


def activated(gathered, channels, h):
    value = gathered[h, :channels, :].astype(f32)
    return (value / (1.0 + jnp.exp(-value))).astype(bf16).astype(f32)


def pack_body(pixels, upstream, outgoing, staged, arrived):
    strips, channels = outgoing.shape[0], pixels.shape[0]
    loads = [
        pltpu.make_async_copy(pixels, staged.at[:channels, :], arrived.at[0]),
        pltpu.make_async_copy(upstream, staged.at[channels:, :], arrived.at[1]),
    ]
    for load in loads:
        load.start()
    for load in loads:
        load.wait()
    quarter = channels // strips
    for strip in range(strips):
        outgoing[strip, :channels, :] = staged[:channels, :]
        outgoing[strip, channels:, :] = staged[
            channels + strip * quarter : channels + (strip + 1) * quarter, :
        ]


def split_body(master, first_moment, second_moment, pieces, *, step):
    state = jnp.concatenate([master[...], first_moment[...], second_moment[...]], axis=0)
    terms = []
    for _ in range(TERMS):
        term = state.astype(bf16).astype(f32)
        terms.append(term)
        state = state - term
    terms = jnp.concatenate(terms, axis=0)
    halves, height, padded = pieces.shape
    excess = (halves - 1) * step + padded - terms.shape[1]
    terms = jnp.concatenate([terms, jnp.zeros((height, excess), f32)], axis=1)
    for half in range(halves):
        pieces[half] = terms[:, half * step : half * step + padded].astype(bf16)


def gradient_body(core, gathered, pieces, kept, sent, cols, *, channels, step):
    rows = gathered.shape[0]
    quarter = gathered.shape[1] - channels
    fill(cols, rows, functools.partial(activated, gathered, channels), 1)
    whole = len(taps) * channels
    if cols.shape[0] > whole:
        cols[whole:, :] = jnp.zeros((cols.shape[0] - whole, cols.shape[1]), bf16)
    upstream = jnp.concatenate([gathered[h, channels:, :] for h in range(rows)], axis=1)
    padded = kept.shape[1]
    for target, half in ((sent, 1 - core[0]), (kept, core[0])):
        start = pl.multiple_of(half * step, 8)
        product = dot(upstream, cols[pl.ds(start, padded), :], 1, 1)
        target[:quarter, :] = product.astype(bf16)
        target[quarter:, :] = pieces[half]


def convolution_body(
    strip, gathered, residual, weight, turned, *results, channels
):
    *results, cols, back_cols, whole = results
    rows, quarter, width = residual.shape
    fill(cols, rows, functools.partial(activated, gathered, channels), 1)
    convolved = dot(weight[...], cols[...], 1, 0)
    for h in range(rows):
        whole[h, :quarter, :] = (
            residual[h].astype(f32) + convolved[:, h * width : (h + 1) * width]
        ).astype(bf16)
    fill(back_cols, rows, lambda h: gathered[h, channels:, :].astype(f32), -1)
    spread = dot(turned[...], back_cols[...], 1, 0)
    for h in range(rows):
        whole[h, quarter:, :] = spread[:, h * width : (h + 1) * width].astype(bf16)
    for ahead, result in enumerate(results):
        target = strip[0] + ahead
        result[...] = whole[jnp.where(target >= rows, target - rows, target)]


def collect_body(strip, pixels, upstream, *pieces, quarter):
    *pieces, output, grad_input = pieces
    strips = len(pieces)
    spread = jnp.zeros(pixels.shape, f32)
    for behind, piece in enumerate(pieces):
        source = strip[0] - behind
        source = jnp.where(source < 0, source + strips, source)
        output[pl.ds(pl.multiple_of(source * quarter, quarter), quarter), :] = piece[:quarter, :]
        spread = spread + piece[quarter:, :].astype(f32)
    value = pixels[...].astype(f32)
    sigmoid = 1.0 / (1.0 + jnp.exp(-value))
    derivative = sigmoid * (1.0 + value * (1.0 - sigmoid))
    grad_input[...] = (upstream[...].astype(f32) + spread * derivative).astype(bf16)


def turn_body(core, kept, received, message, *, quarter):
    ours, others = kept[...].astype(f32), received[...].astype(f32)
    first = core[0] == 0
    rows = [
        ours[:quarter] + others[:quarter],
        jnp.where(first, ours[quarter:], others[quarter:]),
        jnp.where(first, others[quarter:], ours[quarter:]),
    ]
    spare = LANES - 2 * ours.shape[0] + quarter
    if spare:
        rows.append(jnp.zeros((spare, ours.shape[1]), f32))
    turned = jnp.transpose(jnp.concatenate(rows, axis=0))
    chips, chunk, _ = message.shape
    for chip in range(chips):
        message[chip] = turned[chip * chunk : (chip + 1) * chunk, :].astype(bf16)


def adam(grads, master, first_moment, second_moment):
    first_new = beta_first * first_moment + (1.0 - beta_first) * grads
    second_new = beta_second * second_moment + (1.0 - beta_second) * grads * grads
    update = learn_rate * (first_new / bias_first) / (jnp.sqrt(second_new / bias_second) + epsilon)
    return master - update, first_new, second_new


def publish_body(strip, received, slots, message, *, quarter, capacity, halves, cores, root):
    chips, chunk, _ = received.shape
    places = message.shape[0]
    strips = slots.shape[0]
    columns = max(LANES, chips * cores * capacity)
    mine = slots[0:1, :]
    for other in range(1, strips):
        mine = jnp.where(strip[0] == other, slots[other : other + 1, :], mine)
    wide = jnp.concatenate([mine] * 3, axis=1)
    owner, slot = wide // capacity, wide % capacity
    source = owner // cores % halves * places + owner // (halves * cores)
    share = TERMS * 3 * capacity
    row = lax.broadcasted_iota(jnp.int32, (LANES, 3 * LANES), 0) - quarter
    array = lax.broadcasted_iota(jnp.int32, (LANES, 3 * LANES), 1) // LANES
    within = row % (3 * capacity)
    here = (row >= 0) & (row < cores * share) & (wide >= 0) & (row // share == owner % cores)
    here = here & (within // capacity == array) & (within % capacity == slot)
    here = jnp.where(here, 1.0, 0.0).astype(bf16)
    values = [received[chip].astype(f32) for chip in range(chips)]
    grads = values[0]
    for value in values[1:]:
        grads = grads + value
    picked = dot(jnp.concatenate(values, axis=0).astype(bf16), here, 1, 0)
    state = jnp.zeros((chunk, 3 * LANES), f32)
    for chip in range(chips):
        state = jnp.where(source == chip, picked[chip * chunk : (chip + 1) * chunk], state)
    fresh, _, _ = adam(
        grads / root, state[:, :LANES], state[:, LANES : 2 * LANES], state[:, 2 * LANES :]
    )
    index = lax.broadcasted_iota(jnp.int32, (columns, LANES), 0)
    matches = jnp.where(index == mine, 1.0, 0.0).astype(bf16)
    chosen = dot(grads.astype(bf16), matches, 1, 1)
    lane = lax.broadcasted_iota(jnp.int32, (chunk, LANES), 1)
    span = halves * cores * capacity
    per_tile = LANES // span
    for place in range(places):
        tile = chosen[:, place // per_tile * LANES : (place // per_tile + 1) * LANES]
        shift = (quarter - span * (place % per_tile)) % LANES
        moved = tile if shift == 0 else pltpu.roll(tile, shift, 1)
        value = jnp.where(lane < quarter, fresh, jnp.where(lane < quarter + span, moved, 0.0))
        message[place] = value.astype(bf16)


def flat(messages):
    chips, chunk, _ = messages.shape
    return messages[...].astype(f32).reshape(chips * chunk, LANES)


def unit(rows, first):
    shape = (rows, LANES)
    row = lax.broadcasted_iota(jnp.int32, shape, 0)
    return jnp.where(row + first == lax.broadcasted_iota(jnp.int32, shape, 1), 1.0, 0.0).astype(
        bf16
    )


def owned_body(near, message, *, quarter, capacity, strips):
    targets = message.shape[0]
    turned = dot(unit(targets // strips * capacity, quarter), flat(near).astype(bf16), 1, 1)
    for target in range(targets):
        first = target // strips * capacity
        message[target] = turned[first : first + capacity].astype(bf16)


def valid(blocks, halves, step):
    size = blocks // halves
    return [min(size, step - half * size) for half in range(halves)]


def collect_weight_body(seat, *refs, halves, step):
    *shares, new_weight = refs
    quarter = new_weight.shape[0]
    seats = len(shares)
    shares = [flat(share) for share in shares]
    sizes = valid(shares[0].shape[0] * halves, halves, step)
    rows = []
    for core in range(seats // halves):
        for half in range(halves):
            target = half * (seats // halves) + core
            block = shares[0]
            for other in range(1, seats):
                block = jnp.where(seat[0] == target ^ other, shares[other], block)
            rows.append(block[: sizes[half]])
    rows = jnp.concatenate(rows, axis=0).astype(bf16)
    new_weight[...] = dot(unit(quarter, 0), rows, 1, 1).astype(bf16)


def finish_body(
    owned, master, first_moment, second_moment, filled,
    new_master, new_first, new_second, *, halves, step, strips, root,
):
    seats, size = owned.shape[0] // strips, owned.shape[2]
    sizes = valid(size * halves, halves, step)
    blocks = []
    for core in range(seats // halves):
        for half in range(halves):
            first = (half * (seats // halves) + core) * strips
            total = owned[first].astype(f32)
            for strip in range(1, strips):
                total = total + owned[first + strip].astype(f32)
            blocks.append(total[:, : sizes[half]])
    grads = jnp.concatenate(blocks, axis=1) / root
    fresh, first_new, second_new = adam(
        grads, master[...], first_moment[...], second_moment[...]
    )
    keep = filled[...] > 0.0
    new_master[...] = jnp.where(keep, fresh, master[...])
    new_first[...] = jnp.where(keep, first_new, first_moment[...])
    new_second[...] = jnp.where(keep, second_new, second_moment[...])


def slot_tables(owner_list, capacity):
    count = owner_list.shape[0]
    same_owner = owner_list[:, None] == owner_list[None, :]
    order = jnp.arange(count, dtype=jnp.int32)
    earlier = order[None, :] < order[:, None]
    return owner_list * capacity + jnp.sum((same_owner & earlier).astype(jnp.int32), axis=1)


def exchange(value, axes):
    return lax.all_to_all(value, axes, 0, 0, tiled=True)


def local(latents, cotangent, weight, master, first_moment, second_moment, owner_list):
    lines, columns, halves, cores, strips = (
        lax.axis_size(axis) for axis in ("line", "column", "half", "core", "strip")
    )
    places = lines * columns
    seats = halves * cores
    chips = places * halves
    ranks = chips * cores
    strip, core = lax.axis_index("strip"), lax.axis_index("core")
    seat = lax.axis_index("half") * cores + core
    rank = (lax.axis_index("line") * columns + lax.axis_index("column")) * seats + seat
    strip_scalar = strip.reshape(1).astype(jnp.int32)
    core_scalar = core.reshape(1).astype(jnp.int32)
    swap = [(i, cores - 1 - i) for i in range(cores)]
    channels, width = latents.shape[2:]
    quarter = channels // strips
    capacity = master.shape[0]
    height = TERMS * 3 * capacity
    taken = len(taps) * channels
    step = taken // cores
    padded = -(-step // LANES) * LANES
    chunk = padded // chips
    rows = strips
    root = float(ranks * rows * width) ** 0.5
    pixels, upstream = latents[0, 0], cotangent[0, 0]

    outgoing = pl.pallas_call(
        pack_body,
        out_shape=jax.ShapeDtypeStruct((strips, channels + quarter, width), bf16),
        in_specs=[pl.BlockSpec(memory_space=pltpu.HBM)] * 2,
        scratch_shapes=[
            pltpu.VMEM((2 * channels, width), bf16),
            pltpu.SemaphoreType.DMA((2,)),
        ],
        name="pack",
        interpret=interpret,
        compiler_params=pltpu.CompilerParams(vmem_limit_bytes=60 << 20),
    )(pixels, upstream)
    gathered = exchange(outgoing, "strip")

    slot_ids = slot_tables(owner_list, capacity)
    slots = jnp.pad(
        slot_ids.reshape(strips, quarter), ((0, 0), (0, LANES - quarter)), constant_values=-1
    )
    owned = jnp.sum((owner_list == rank).astype(jnp.int32))
    filled = (jnp.arange(capacity, dtype=jnp.int32) < owned).astype(f32)[:, None]
    turned = weight.reshape(quarter, len(taps), channels).transpose(2, 1, 0)
    turned = turned.reshape(channels, len(taps) * quarter)
    pieces = call(
        functools.partial(split_body, step=step),
        jax.ShapeDtypeStruct((cores, height, padded), bf16),
    )(master, first_moment, second_moment)
    gathered, slots, filled, turned, pieces = lax.optimization_barrier(
        (gathered, slots, filled, turned, pieces)
    )

    kept, sent = call(
        functools.partial(gradient_body, channels=channels, step=step),
        [jax.ShapeDtypeStruct((quarter + height, padded), bf16)] * 2,
        [pltpu.VMEM(((cores - 1) * step + padded, rows * width), bf16)],
        scalars=1,
        inputs=2,
    )(core_scalar, gathered, pieces)
    swapped = lax.ppermute(sent, "core", swap)

    residual = lax.dynamic_slice_in_dim(gathered, strip * quarter, quarter, axis=1)
    results = call(
        functools.partial(convolution_body, channels=channels),
        [jax.ShapeDtypeStruct((quarter + channels, width), bf16)] * strips,
        [
            pltpu.VMEM((taken, rows * width), bf16),
            pltpu.VMEM((len(taps) * quarter, rows * width), bf16),
            pltpu.VMEM((rows, quarter + channels, width), bf16),
        ],
        scalars=1,
        inputs=4,
    )(strip_scalar, gathered, residual, weight, turned)

    returned = [results[0]]
    for ahead in range(1, strips):
        pairs = [(i, (i + ahead) % strips) for i in range(strips)]
        returned.append(lax.ppermute(results[ahead], "strip", pairs))

    by_chip = call(
        functools.partial(turn_body, quarter=quarter),
        jax.ShapeDtypeStruct((chips, chunk, LANES), bf16),
        scalars=1,
        inputs=2,
    )(core_scalar, kept, swapped)
    by_chip = exchange(by_chip, ("half", "line", "column"))
    message = call(
        functools.partial(
            publish_body, quarter=quarter, capacity=capacity, halves=halves, cores=cores,
            root=root,
        ),
        jax.ShapeDtypeStruct((places, chunk, LANES), bf16),
        scalars=1,
        inputs=2,
    )(strip_scalar, by_chip, slots)
    near = exchange(message, ("line", "column"))

    output, grad_input = call(
        functools.partial(collect_body, quarter=quarter),
        [jax.ShapeDtypeStruct((channels, width), bf16)] * 2,
        scalars=1,
        inputs=2 + strips,
    )(strip_scalar, pixels, upstream, *returned)

    shares = [near]
    for other in range(1, seats):
        pairs = [(i, i ^ other) for i in range(seats)]
        shares.append(lax.ppermute(near, ("half", "core"), pairs))
    owned_rows = call(
        functools.partial(owned_body, quarter=quarter, capacity=capacity, strips=strips),
        jax.ShapeDtypeStruct((seats * strips, capacity, places * chunk), bf16),
    )(near)
    owned_rows = exchange(owned_rows, ("half", "core", "strip"))
    new_weight = call(
        functools.partial(collect_weight_body, halves=halves, step=step),
        jax.ShapeDtypeStruct((quarter, taken), bf16),
        scalars=1,
        inputs=seats,
    )(seat.reshape(1).astype(jnp.int32), *shares)
    new_master, new_first, new_second = call(
        functools.partial(finish_body, halves=halves, step=step, strips=strips, root=root),
        [jax.ShapeDtypeStruct(master.shape, f32)] * 3,
    )(owned_rows, master, first_moment, second_moment, filled)
    return (output[None, None], grad_input[None, None], new_weight, new_master, new_first, new_second)


def solution(mesh):
    fine = Mesh(
        mesh.devices.reshape(RANK_SHAPE + (mesh.shape["strip"],)),
        ("line", "column", "half", "core", "strip"),
    )
    ranks = ("line", "column", "half", "core")
    images = P(ranks, "strip", None, None)
    specs = (images, images, P("strip", None), P(ranks, None), P(ranks, None), P(ranks, None))

    return jax.shard_map(
        local, mesh=fine, in_specs=specs + (P(),), out_specs=specs, check_vma=False
    )
```

```python
import functools
import jax
import jax.numpy as jnp
from jax import lax
from jax.experimental import pallas as pl
from jax.experimental.pallas import tpu as pltpu
from jax.sharding import Mesh, PartitionSpec as P

beta_first = 0.9
beta_second = 0.999
learn_rate = 0.01
epsilon = 1e-08
bias_first = 1.0 - 0.9**10
bias_second = 1.0 - 0.999**10

interpret = False
LANES = 128
RANK_SHAPE = (8, 8, 2)
TERMS = 2
taps = [(dh, dw) for dh in (-1, 0, 1) for dw in (-1, 0, 1)]
f32 = jnp.float32
bf16 = jnp.bfloat16


def call(body, out_shape, scratch=(), scalars=0, inputs=0):
    specs = {}
    if scalars:
        specs["in_specs"] = [pl.BlockSpec(memory_space=pltpu.SMEM)] * scalars + [
            pl.BlockSpec(memory_space=pltpu.VMEM)
        ] * inputs
    return pl.pallas_call(
        body,
        out_shape=out_shape,
        scratch_shapes=scratch,
        interpret=interpret,
        compiler_params=pltpu.CompilerParams(vmem_limit_bytes=20 << 20),
        **specs,
    )


def dot(left, right, left_dim, right_dim):
    return lax.dot_general(
        left, right, (((left_dim,), (right_dim,)), ((), ())), preferred_element_type=f32
    )


def shifted(value):
    lane = lax.broadcasted_iota(jnp.int32, value.shape, 1)
    last = value.shape[1] - 1
    before = jnp.where(lane == 0, 0.0, pltpu.roll(value, 1, 1))
    after = jnp.where(lane == last, 0.0, pltpu.roll(value, last, 1))
    return {-1: before.astype(bf16), 0: value.astype(bf16), 1: after.astype(bf16)}


def fill(cols, rows, load, direction):
    first = load(0)
    count, width = first.shape
    for index, (dh, _) in enumerate(taps):
        for h in range(rows):
            if not 0 <= h + direction * dh < rows:
                cols[index * count : (index + 1) * count, h * width : (h + 1) * width] = jnp.zeros(
                    (count, width), bf16
                )
    for source in range(rows):
        versions = shifted(first if source == 0 else load(source))
        for index, (dh, dw) in enumerate(taps):
            h = source - direction * dh
            if 0 <= h < rows:
                cols[index * count : (index + 1) * count, h * width : (h + 1) * width] = versions[
                    direction * dw
                ]


def activated(gathered, channels, h):
    value = gathered[h, :channels, :].astype(f32)
    return (value / (1.0 + jnp.exp(-value))).astype(bf16).astype(f32)


def pack_body(pixels, upstream, outgoing, staged, arrived):
    strips, channels = outgoing.shape[0], pixels.shape[0]
    loads = [
        pltpu.make_async_copy(pixels, staged.at[:channels, :], arrived.at[0]),
        pltpu.make_async_copy(upstream, staged.at[channels:, :], arrived.at[1]),
    ]
    for load in loads:
        load.start()
    for load in loads:
        load.wait()
    quarter = channels // strips
    for strip in range(strips):
        outgoing[strip, :channels, :] = staged[:channels, :]
        outgoing[strip, channels:, :] = staged[
            channels + strip * quarter : channels + (strip + 1) * quarter, :
        ]


def split_body(master, first_moment, second_moment, pieces, *, step):
    state = jnp.concatenate([master[...], first_moment[...], second_moment[...]], axis=0)
    terms = []
    for _ in range(TERMS):
        term = state.astype(bf16).astype(f32)
        terms.append(term)
        state = state - term
    terms = jnp.concatenate(terms, axis=0)
    halves, height, padded = pieces.shape
    excess = (halves - 1) * step + padded - terms.shape[1]
    terms = jnp.concatenate([terms, jnp.zeros((height, excess), f32)], axis=1)
    for half in range(halves):
        pieces[half] = terms[:, half * step : half * step + padded].astype(bf16)


def gradient_body(core, gathered, pieces, target, cols, *, channels, step, other):
    rows = gathered.shape[0]
    quarter = gathered.shape[1] - channels
    fill(cols, rows, functools.partial(activated, gathered, channels), 1)
    whole = len(taps) * channels
    if cols.shape[0] > whole:
        cols[whole:, :] = jnp.zeros((cols.shape[0] - whole, cols.shape[1]), bf16)
    upstream = jnp.concatenate([gathered[h, channels:, :] for h in range(rows)], axis=1)
    half = 1 - core[0] if other else core[0]
    start = pl.multiple_of(half * step, 8)
    product = dot(upstream, cols[pl.ds(start, target.shape[1]), :], 1, 1)
    target[:quarter, :] = product.astype(bf16)
    target[quarter:, :] = pieces[half]


def convolution_body(
    strip, gathered, residual, weight, turned, *results, channels
):
    *results, cols, back_cols, whole = results
    rows, quarter, width = residual.shape
    fill(cols, rows, functools.partial(activated, gathered, channels), 1)
    convolved = dot(weight[...], cols[...], 1, 0)
    for h in range(rows):
        whole[h, :quarter, :] = (
            residual[h].astype(f32) + convolved[:, h * width : (h + 1) * width]
        ).astype(bf16)
    fill(back_cols, rows, lambda h: gathered[h, channels:, :].astype(f32), -1)
    spread = dot(turned[...], back_cols[...], 1, 0)
    for h in range(rows):
        whole[h, quarter:, :] = spread[:, h * width : (h + 1) * width].astype(bf16)
    for ahead, result in enumerate(results):
        target = strip[0] + ahead
        result[...] = whole[jnp.where(target >= rows, target - rows, target)]


def collect_body(strip, pixels, upstream, *pieces, quarter):
    *pieces, output, grad_input = pieces
    strips = len(pieces)
    spread = jnp.zeros(pixels.shape, f32)
    for behind, piece in enumerate(pieces):
        source = strip[0] - behind
        source = jnp.where(source < 0, source + strips, source)
        output[pl.ds(pl.multiple_of(source * quarter, quarter), quarter), :] = piece[:quarter, :]
        spread = spread + piece[quarter:, :].astype(f32)
    value = pixels[...].astype(f32)
    sigmoid = 1.0 / (1.0 + jnp.exp(-value))
    derivative = sigmoid * (1.0 + value * (1.0 - sigmoid))
    grad_input[...] = (upstream[...].astype(f32) + spread * derivative).astype(bf16)


def turn_body(core, kept, received, message, *, quarter):
    ours, others = kept[...].astype(f32), received[...].astype(f32)
    first = core[0] == 0
    rows = [
        ours[:quarter] + others[:quarter],
        jnp.where(first, ours[quarter:], others[quarter:]),
        jnp.where(first, others[quarter:], ours[quarter:]),
    ]
    spare = LANES - 2 * ours.shape[0] + quarter
    if spare:
        rows.append(jnp.zeros((spare, ours.shape[1]), f32))
    turned = jnp.transpose(jnp.concatenate(rows, axis=0))
    chips, chunk, _ = message.shape
    for chip in range(chips):
        message[chip] = turned[chip * chunk : (chip + 1) * chunk, :].astype(bf16)


def adam(grads, master, first_moment, second_moment):
    first_new = beta_first * first_moment + (1.0 - beta_first) * grads
    second_new = beta_second * second_moment + (1.0 - beta_second) * grads * grads
    update = learn_rate * (first_new / bias_first) / (jnp.sqrt(second_new / bias_second) + epsilon)
    return master - update, first_new, second_new


def publish_body(strip, received, slots, message, *, quarter, capacity, cores, root):
    chips, chunk, _ = received.shape
    strips = slots.shape[0]
    columns = max(LANES, chips * cores * capacity)
    mine = slots[0:1, :]
    for other in range(1, strips):
        mine = jnp.where(strip[0] == other, slots[other : other + 1, :], mine)
    wide = jnp.concatenate([mine] * 3, axis=1)
    owner, place = wide // capacity, wide % capacity
    share = TERMS * 3 * capacity
    row = lax.broadcasted_iota(jnp.int32, (LANES, 3 * LANES), 0) - quarter
    array = lax.broadcasted_iota(jnp.int32, (LANES, 3 * LANES), 1) // LANES
    within = row % (3 * capacity)
    here = (row >= 0) & (row < cores * share) & (wide >= 0) & (row // share == owner % cores)
    here = here & (within // capacity == array) & (within % capacity == place)
    here = jnp.where(here, 1.0, 0.0).astype(bf16)
    values = [received[chip].astype(f32) for chip in range(chips)]
    grads = values[0]
    for value in values[1:]:
        grads = grads + value
    picked = dot(jnp.concatenate(values, axis=0).astype(bf16), here, 1, 0)
    state = jnp.zeros((chunk, 3 * LANES), f32)
    for chip in range(chips):
        state = jnp.where(
            owner // cores == chip, picked[chip * chunk : (chip + 1) * chunk], state
        )
    fresh, _, _ = adam(
        grads / root, state[:, :LANES], state[:, LANES : 2 * LANES], state[:, 2 * LANES :]
    )
    index = lax.broadcasted_iota(jnp.int32, (columns, LANES), 0)
    matches = jnp.where(index == mine, 1.0, 0.0).astype(bf16)
    chosen = dot(grads.astype(bf16), matches, 1, 1)
    lane = lax.broadcasted_iota(jnp.int32, (chunk, LANES), 1)
    span = cores * capacity
    per_tile = LANES // span
    for chip in range(chips):
        tile = chosen[:, chip // per_tile * LANES : (chip // per_tile + 1) * LANES]
        shift = (quarter - span * (chip % per_tile)) % LANES
        moved = tile if shift == 0 else pltpu.roll(tile, shift, 1)
        value = jnp.where(lane < quarter, fresh, jnp.where(lane < quarter + span, moved, 0.0))
        message[chip] = value.astype(bf16)


def flat(messages):
    chips, chunk, _ = messages.shape
    return messages[...].astype(f32).reshape(chips * chunk, LANES)


def unit(rows, first):
    shape = (rows, LANES)
    row = lax.broadcasted_iota(jnp.int32, shape, 0)
    return jnp.where(row + first == lax.broadcasted_iota(jnp.int32, shape, 1), 1.0, 0.0).astype(
        bf16
    )


def owned_body(near, message, *, quarter, capacity, strips):
    targets = message.shape[0]
    turned = dot(unit(16, quarter), flat(near).astype(bf16), 1, 1)
    for target in range(targets):
        first = target // strips * capacity
        message[target] = turned[first : first + capacity].astype(bf16)


def collect_weight_body(core, near, far, new_weight, *, step):
    ours, others = flat(near), flat(far)
    first = core[0] == 0
    rows = [jnp.where(first, ours, others)[:step], jnp.where(first, others, ours)[:step]]
    rows = jnp.concatenate(rows, axis=0).astype(bf16)
    new_weight[...] = dot(unit(new_weight.shape[0], 0), rows, 1, 1).astype(bf16)


def finish_body(
    owned, master, first_moment, second_moment, filled,
    new_master, new_first, new_second, *, step, strips, root,
):
    halves = []
    for half in range(owned.shape[0] // strips):
        total = owned[half * strips].astype(f32)
        for strip in range(1, strips):
            total = total + owned[half * strips + strip].astype(f32)
        halves.append(total[:, :step])
    grads = jnp.concatenate(halves, axis=1) / root
    fresh, first_new, second_new = adam(
        grads, master[...], first_moment[...], second_moment[...]
    )
    keep = filled[...] > 0.0
    new_master[...] = jnp.where(keep, fresh, master[...])
    new_first[...] = jnp.where(keep, first_new, first_moment[...])
    new_second[...] = jnp.where(keep, second_new, second_moment[...])


def slot_tables(owner_list, capacity):
    count = owner_list.shape[0]
    same_owner = owner_list[:, None] == owner_list[None, :]
    order = jnp.arange(count, dtype=jnp.int32)
    earlier = order[None, :] < order[:, None]
    return owner_list * capacity + jnp.sum((same_owner & earlier).astype(jnp.int32), axis=1)


def exchange(value, axes):
    return lax.all_to_all(value, axes, 0, 0, tiled=True)


def local(latents, cotangent, weight, master, first_moment, second_moment, owner_list):
    lines, groups, cores, strips = (lax.axis_size(a) for a in ("line", "group", "core", "strip"))
    chips = lines * groups
    ranks = chips * cores
    strip, core = lax.axis_index("strip"), lax.axis_index("core")
    rank = (lax.axis_index("line") * groups + lax.axis_index("group")) * cores + core
    strip_scalar = strip.reshape(1).astype(jnp.int32)
    core_scalar = core.reshape(1).astype(jnp.int32)
    swap = [(i, cores - 1 - i) for i in range(cores)]
    channels, width = latents.shape[2:]
    quarter = channels // strips
    capacity = master.shape[0]
    height = TERMS * 3 * capacity
    taken = len(taps) * channels
    step = taken // cores
    padded = -(-step // LANES) * LANES
    chunk = padded // chips
    rows = strips
    root = float(ranks * rows * width) ** 0.5
    pixels, upstream = latents[0, 0], cotangent[0, 0]

    outgoing = pl.pallas_call(
        pack_body,
        out_shape=jax.ShapeDtypeStruct((strips, channels + quarter, width), bf16),
        in_specs=[pl.BlockSpec(memory_space=pltpu.HBM)] * 2,
        scratch_shapes=[
            pltpu.VMEM((2 * channels, width), bf16),
            pltpu.SemaphoreType.DMA((2,)),
        ],
        name="pack",
        interpret=interpret,
        compiler_params=pltpu.CompilerParams(vmem_limit_bytes=60 << 20),
    )(pixels, upstream)
    gathered = exchange(outgoing, "strip")

    slot_ids = slot_tables(owner_list, capacity)
    slots = jnp.pad(
        slot_ids.reshape(strips, quarter), ((0, 0), (0, LANES - quarter)), constant_values=-1
    )
    owned = jnp.sum((owner_list == rank).astype(jnp.int32))
    filled = (jnp.arange(capacity, dtype=jnp.int32) < owned).astype(f32)[:, None]
    turned = weight.reshape(quarter, len(taps), channels).transpose(2, 1, 0)
    turned = turned.reshape(channels, len(taps) * quarter)
    pieces = call(
        functools.partial(split_body, step=step),
        jax.ShapeDtypeStruct((cores, height, padded), bf16),
    )(master, first_moment, second_moment)
    gathered, slots, filled, turned, pieces = lax.optimization_barrier(
        (gathered, slots, filled, turned, pieces)
    )

    sent, kept = (
        call(
            functools.partial(gradient_body, channels=channels, step=step, other=other),
            jax.ShapeDtypeStruct((quarter + height, padded), bf16),
            [pltpu.VMEM(((cores - 1) * step + padded, rows * width), bf16)],
            scalars=1,
            inputs=2,
        )(core_scalar, gathered, pieces)
        for other in (True, False)
    )
    swapped = lax.ppermute(sent, "core", swap)

    residual = lax.dynamic_slice_in_dim(gathered, strip * quarter, quarter, axis=1)
    results = call(
        functools.partial(convolution_body, channels=channels),
        [jax.ShapeDtypeStruct((quarter + channels, width), bf16)] * strips,
        [
            pltpu.VMEM((taken, rows * width), bf16),
            pltpu.VMEM((len(taps) * quarter, rows * width), bf16),
            pltpu.VMEM((rows, quarter + channels, width), bf16),
        ],
        scalars=1,
        inputs=4,
    )(strip_scalar, gathered, residual, weight, turned)

    returned = [results[0]]
    for ahead in range(1, strips):
        pairs = [(i, (i + ahead) % strips) for i in range(strips)]
        returned.append(lax.ppermute(results[ahead], "strip", pairs))

    by_chip = call(
        functools.partial(turn_body, quarter=quarter),
        jax.ShapeDtypeStruct((chips, chunk, LANES), bf16),
        scalars=1,
        inputs=2,
    )(core_scalar, kept, swapped)
    by_chip = exchange(by_chip, ("line", "group"))
    message = call(
        functools.partial(publish_body, quarter=quarter, capacity=capacity, cores=cores, root=root),
        jax.ShapeDtypeStruct((chips, chunk, LANES), bf16),
        scalars=1,
        inputs=2,
    )(strip_scalar, by_chip, slots)
    near = exchange(message, ("line", "group"))

    output, grad_input = call(
        functools.partial(collect_body, quarter=quarter),
        [jax.ShapeDtypeStruct((channels, width), bf16)] * 2,
        scalars=1,
        inputs=2 + strips,
    )(strip_scalar, pixels, upstream, *returned)

    far = lax.ppermute(near, "core", swap)
    owned_rows = call(
        functools.partial(owned_body, quarter=quarter, capacity=capacity, strips=strips),
        jax.ShapeDtypeStruct((cores * strips, capacity, padded), bf16),
    )(near)
    owned_rows = exchange(owned_rows, ("core", "strip"))
    new_weight = call(
        functools.partial(collect_weight_body, step=step),
        jax.ShapeDtypeStruct((quarter, taken), bf16),
        scalars=1,
        inputs=2,
    )(core_scalar, near, far)
    owned_rows, new_weight = lax.optimization_barrier((owned_rows, new_weight))
    new_master, new_first, new_second = call(
        functools.partial(finish_body, step=step, strips=strips, root=root),
        [jax.ShapeDtypeStruct(master.shape, f32)] * 3,
    )(owned_rows, master, first_moment, second_moment, filled)
    return (output[None, None], grad_input[None, None], new_weight, new_master, new_first, new_second)


def solution(mesh):
    fine = Mesh(
        mesh.devices.reshape(RANK_SHAPE + (mesh.shape["strip"],)),
        ("line", "group", "core", "strip"),
    )
    ranks = ("line", "group", "core")
    images = P(ranks, "strip", None, None)
    specs = (images, images, P("strip", None), P(ranks, None), P(ranks, None), P(ranks, None))

    return jax.shard_map(
        local, mesh=fine, in_specs=specs + (P(),), out_specs=specs, check_vma=False
    )
```

```python
import functools
import jax
import jax.numpy as jnp
from jax import lax
from jax.experimental import pallas as pl
from jax.experimental.pallas import tpu as pltpu
from jax.sharding import Mesh, PartitionSpec as P

beta_first = 0.9
beta_second = 0.999
learn_rate = 0.01
epsilon = 1e-08
bias_first = 1.0 - 0.9**10
bias_second = 1.0 - 0.999**10

interpret = False
LANES = 128
RANK_SHAPE = (8, 8, 2)
TERMS = 2
taps = [(dh, dw) for dh in (-1, 0, 1) for dw in (-1, 0, 1)]
f32 = jnp.float32
bf16 = jnp.bfloat16


def call(body, out_shape, scratch=(), scalars=0, inputs=0):
    specs = {}
    if scalars:
        specs["in_specs"] = [pl.BlockSpec(memory_space=pltpu.SMEM)] * scalars + [
            pl.BlockSpec(memory_space=pltpu.VMEM)
        ] * inputs
    return pl.pallas_call(
        body,
        out_shape=out_shape,
        scratch_shapes=scratch,
        interpret=interpret,
        compiler_params=pltpu.CompilerParams(vmem_limit_bytes=20 << 20),
        **specs,
    )


def dot(left, right, left_dim, right_dim):
    return lax.dot_general(
        left, right, (((left_dim,), (right_dim,)), ((), ())), preferred_element_type=f32
    )


def shifted(value):
    lane = lax.broadcasted_iota(jnp.int32, value.shape, 1)
    last = value.shape[1] - 1
    before = jnp.where(lane == 0, 0.0, pltpu.roll(value, 1, 1))
    after = jnp.where(lane == last, 0.0, pltpu.roll(value, last, 1))
    return {-1: before.astype(bf16), 0: value.astype(bf16), 1: after.astype(bf16)}


def fill(cols, rows, load, direction):
    first = load(0)
    count, width = first.shape
    for index, (dh, _) in enumerate(taps):
        for h in range(rows):
            if not 0 <= h + direction * dh < rows:
                cols[index * count : (index + 1) * count, h * width : (h + 1) * width] = jnp.zeros(
                    (count, width), bf16
                )
    for source in range(rows):
        versions = shifted(first if source == 0 else load(source))
        for index, (dh, dw) in enumerate(taps):
            h = source - direction * dh
            if 0 <= h < rows:
                cols[index * count : (index + 1) * count, h * width : (h + 1) * width] = versions[
                    direction * dw
                ]


def activated(gathered, channels, h):
    value = gathered[h, :channels, :].astype(f32)
    return (value / (1.0 + jnp.exp(-value))).astype(bf16).astype(f32)


def pack_body(pixels, upstream, outgoing, staged, arrived):
    strips, channels = outgoing.shape[0], pixels.shape[0]
    loads = [
        pltpu.make_async_copy(pixels, staged.at[:channels, :], arrived.at[0]),
        pltpu.make_async_copy(upstream, staged.at[channels:, :], arrived.at[1]),
    ]
    for load in loads:
        load.start()
    for load in loads:
        load.wait()
    quarter = channels // strips
    for strip in range(strips):
        outgoing[strip, :channels, :] = staged[:channels, :]
        outgoing[strip, channels:, :] = staged[
            channels + strip * quarter : channels + (strip + 1) * quarter, :
        ]


def split_body(master, first_moment, second_moment, pieces, *, step):
    state = jnp.concatenate([master[...], first_moment[...], second_moment[...]], axis=0)
    terms = []
    for _ in range(TERMS):
        term = state.astype(bf16).astype(f32)
        terms.append(term)
        state = state - term
    terms = jnp.concatenate(terms, axis=0)
    halves, height, padded = pieces.shape
    excess = (halves - 1) * step + padded - terms.shape[1]
    terms = jnp.concatenate([terms, jnp.zeros((height, excess), f32)], axis=1)
    for half in range(halves):
        pieces[half] = terms[:, half * step : half * step + padded].astype(bf16)


def gradient_body(core, gathered, pieces, target, cols, *, channels, step, other):
    rows = gathered.shape[0]
    quarter = gathered.shape[1] - channels
    fill(cols, rows, functools.partial(activated, gathered, channels), 1)
    whole = len(taps) * channels
    if cols.shape[0] > whole:
        cols[whole:, :] = jnp.zeros((cols.shape[0] - whole, cols.shape[1]), bf16)
    upstream = jnp.concatenate([gathered[h, channels:, :] for h in range(rows)], axis=1)
    half = 1 - core[0] if other else core[0]
    start = pl.multiple_of(half * step, 8)
    product = dot(upstream, cols[pl.ds(start, target.shape[1]), :], 1, 1)
    target[:quarter, :] = product.astype(bf16)
    target[quarter:, :] = pieces[half]


def convolution_body(
    strip, gathered, residual, weight, turned, *results, channels
):
    *results, cols, back_cols, whole = results
    rows, quarter, width = residual.shape
    fill(cols, rows, functools.partial(activated, gathered, channels), 1)
    convolved = dot(weight[...], cols[...], 1, 0)
    for h in range(rows):
        whole[h, :quarter, :] = (
            residual[h].astype(f32) + convolved[:, h * width : (h + 1) * width]
        ).astype(bf16)
    fill(back_cols, rows, lambda h: gathered[h, channels:, :].astype(f32), -1)
    spread = dot(turned[...], back_cols[...], 1, 0)
    for h in range(rows):
        whole[h, quarter:, :] = spread[:, h * width : (h + 1) * width].astype(bf16)
    for ahead, result in enumerate(results):
        target = strip[0] + ahead
        result[...] = whole[jnp.where(target >= rows, target - rows, target)]


def collect_body(strip, pixels, upstream, *pieces, quarter):
    *pieces, output, grad_input = pieces
    strips = len(pieces)
    spread = jnp.zeros(pixels.shape, f32)
    for behind, piece in enumerate(pieces):
        source = strip[0] - behind
        source = jnp.where(source < 0, source + strips, source)
        output[pl.ds(pl.multiple_of(source * quarter, quarter), quarter), :] = piece[:quarter, :]
        spread = spread + piece[quarter:, :].astype(f32)
    value = pixels[...].astype(f32)
    sigmoid = 1.0 / (1.0 + jnp.exp(-value))
    derivative = sigmoid * (1.0 + value * (1.0 - sigmoid))
    grad_input[...] = (upstream[...].astype(f32) + spread * derivative).astype(bf16)


def turn_body(core, kept, received, message, *, quarter):
    ours, others = kept[...].astype(f32), received[...].astype(f32)
    first = core[0] == 0
    rows = [
        ours[:quarter] + others[:quarter],
        jnp.where(first, ours[quarter:], others[quarter:]),
        jnp.where(first, others[quarter:], ours[quarter:]),
    ]
    spare = LANES - 2 * ours.shape[0] + quarter
    if spare:
        rows.append(jnp.zeros((spare, ours.shape[1]), f32))
    turned = jnp.transpose(jnp.concatenate(rows, axis=0))
    chips, chunk, _ = message.shape
    for chip in range(chips):
        message[chip] = turned[chip * chunk : (chip + 1) * chunk, :].astype(bf16)


def adam(grads, master, first_moment, second_moment):
    first_new = beta_first * first_moment + (1.0 - beta_first) * grads
    second_new = beta_second * second_moment + (1.0 - beta_second) * grads * grads
    update = learn_rate * (first_new / bias_first) / (jnp.sqrt(second_new / bias_second) + epsilon)
    return master - update, first_new, second_new


def publish_body(strip, received, slots, message, *, quarter, capacity, groups, cores, root):
    chips, chunk, _ = received.shape
    strips = slots.shape[0]
    columns = max(LANES, chips * cores * capacity)
    mine = slots[0:1, :]
    for other in range(1, strips):
        mine = jnp.where(strip[0] == other, slots[other : other + 1, :], mine)
    wide = jnp.concatenate([mine] * 3, axis=1)
    owner, place = wide // capacity, wide % capacity
    lines = chips // groups
    source = owner // cores % groups * lines + owner // (cores * groups)
    share = TERMS * 3 * capacity
    row = lax.broadcasted_iota(jnp.int32, (LANES, 3 * LANES), 0) - quarter
    array = lax.broadcasted_iota(jnp.int32, (LANES, 3 * LANES), 1) // LANES
    within = row % (3 * capacity)
    here = (row >= 0) & (row < cores * share) & (wide >= 0) & (row // share == owner % cores)
    here = here & (within // capacity == array) & (within % capacity == place)
    here = jnp.where(here, 1.0, 0.0).astype(bf16)
    values = [received[chip].astype(f32) for chip in range(chips)]
    grads = values[0]
    for value in values[1:]:
        grads = grads + value
    picked = dot(jnp.concatenate(values, axis=0).astype(bf16), here, 1, 0)
    state = jnp.zeros((chunk, 3 * LANES), f32)
    for chip in range(chips):
        state = jnp.where(source == chip, picked[chip * chunk : (chip + 1) * chunk], state)
    fresh, _, _ = adam(
        grads / root, state[:, :LANES], state[:, LANES : 2 * LANES], state[:, 2 * LANES :]
    )
    index = lax.broadcasted_iota(jnp.int32, (columns, LANES), 0)
    matches = jnp.where(index == mine, 1.0, 0.0).astype(bf16)
    chosen = dot(grads.astype(bf16), matches, 1, 1)
    lane = lax.broadcasted_iota(jnp.int32, (chunk, LANES), 1)
    span = cores * capacity
    per_tile = LANES // span
    for chip in range(chips):
        number = chip % lines * groups + chip // lines
        tile = chosen[:, number // per_tile * LANES : (number // per_tile + 1) * LANES]
        shift = (quarter - span * (number % per_tile)) % LANES
        moved = tile if shift == 0 else pltpu.roll(tile, shift, 1)
        value = jnp.where(lane < quarter, fresh, jnp.where(lane < quarter + span, moved, 0.0))
        message[chip] = value.astype(bf16)


def flat(messages):
    chips, chunk, _ = messages.shape
    return messages[...].astype(f32).reshape(chips * chunk, LANES)


def unit(rows, first):
    shape = (rows, LANES)
    row = lax.broadcasted_iota(jnp.int32, shape, 0)
    return jnp.where(row + first == lax.broadcasted_iota(jnp.int32, shape, 1), 1.0, 0.0).astype(
        bf16
    )


def owned_body(near, message, *, quarter, capacity, strips):
    targets = message.shape[0]
    turned = dot(unit(16, quarter), flat(near).astype(bf16), 1, 1)
    for target in range(targets):
        first = target // strips * capacity
        message[target] = turned[first : first + capacity].astype(bf16)


def collect_weight_body(core, near, far, new_weight, *, step):
    ours, others = flat(near), flat(far)
    first = core[0] == 0
    rows = [jnp.where(first, ours, others)[:step], jnp.where(first, others, ours)[:step]]
    rows = jnp.concatenate(rows, axis=0).astype(bf16)
    new_weight[...] = dot(unit(new_weight.shape[0], 0), rows, 1, 1).astype(bf16)


def finish_body(
    owned, master, first_moment, second_moment, filled,
    new_master, new_first, new_second, *, step, strips, root,
):
    halves = []
    for half in range(owned.shape[0] // strips):
        total = owned[half * strips].astype(f32)
        for strip in range(1, strips):
            total = total + owned[half * strips + strip].astype(f32)
        halves.append(total[:, :step])
    grads = jnp.concatenate(halves, axis=1) / root
    fresh, first_new, second_new = adam(
        grads, master[...], first_moment[...], second_moment[...]
    )
    keep = filled[...] > 0.0
    new_master[...] = jnp.where(keep, fresh, master[...])
    new_first[...] = jnp.where(keep, first_new, first_moment[...])
    new_second[...] = jnp.where(keep, second_new, second_moment[...])


def slot_tables(owner_list, capacity):
    count = owner_list.shape[0]
    same_owner = owner_list[:, None] == owner_list[None, :]
    order = jnp.arange(count, dtype=jnp.int32)
    earlier = order[None, :] < order[:, None]
    return owner_list * capacity + jnp.sum((same_owner & earlier).astype(jnp.int32), axis=1)


def exchange(value, axes):
    return lax.all_to_all(value, axes, 0, 0, tiled=True)


def local(latents, cotangent, weight, master, first_moment, second_moment, owner_list):
    lines, groups, cores, strips = (lax.axis_size(a) for a in ("line", "group", "core", "strip"))
    chips = lines * groups
    ranks = chips * cores
    strip, core = lax.axis_index("strip"), lax.axis_index("core")
    rank = (lax.axis_index("line") * groups + lax.axis_index("group")) * cores + core
    strip_scalar = strip.reshape(1).astype(jnp.int32)
    core_scalar = core.reshape(1).astype(jnp.int32)
    swap = [(i, cores - 1 - i) for i in range(cores)]
    channels, width = latents.shape[2:]
    quarter = channels // strips
    capacity = master.shape[0]
    height = TERMS * 3 * capacity
    taken = len(taps) * channels
    step = taken // cores
    padded = -(-step // LANES) * LANES
    chunk = padded // chips
    rows = strips
    root = float(ranks * rows * width) ** 0.5
    pixels, upstream = latents[0, 0], cotangent[0, 0]

    outgoing = pl.pallas_call(
        pack_body,
        out_shape=jax.ShapeDtypeStruct((strips, channels + quarter, width), bf16),
        in_specs=[pl.BlockSpec(memory_space=pltpu.HBM)] * 2,
        scratch_shapes=[
            pltpu.VMEM((2 * channels, width), bf16),
            pltpu.SemaphoreType.DMA((2,)),
        ],
        name="pack",
        interpret=interpret,
        compiler_params=pltpu.CompilerParams(vmem_limit_bytes=60 << 20),
    )(pixels, upstream)
    gathered = exchange(outgoing, "strip")

    slot_ids = slot_tables(owner_list, capacity)
    slots = jnp.pad(
        slot_ids.reshape(strips, quarter), ((0, 0), (0, LANES - quarter)), constant_values=-1
    )
    owned = jnp.sum((owner_list == rank).astype(jnp.int32))
    filled = (jnp.arange(capacity, dtype=jnp.int32) < owned).astype(f32)[:, None]
    turned = weight.reshape(quarter, len(taps), channels).transpose(2, 1, 0)
    turned = turned.reshape(channels, len(taps) * quarter)
    pieces = call(
        functools.partial(split_body, step=step),
        jax.ShapeDtypeStruct((cores, height, padded), bf16),
    )(master, first_moment, second_moment)
    gathered, slots, filled, turned, pieces = lax.optimization_barrier(
        (gathered, slots, filled, turned, pieces)
    )

    sent, kept = (
        call(
            functools.partial(gradient_body, channels=channels, step=step, other=other),
            jax.ShapeDtypeStruct((quarter + height, padded), bf16),
            [pltpu.VMEM(((cores - 1) * step + padded, rows * width), bf16)],
            scalars=1,
            inputs=2,
        )(core_scalar, gathered, pieces)
        for other in (True, False)
    )
    swapped = lax.ppermute(sent, "core", swap)

    residual = lax.dynamic_slice_in_dim(gathered, strip * quarter, quarter, axis=1)
    results = call(
        functools.partial(convolution_body, channels=channels),
        [jax.ShapeDtypeStruct((quarter + channels, width), bf16)] * strips,
        [
            pltpu.VMEM((taken, rows * width), bf16),
            pltpu.VMEM((len(taps) * quarter, rows * width), bf16),
            pltpu.VMEM((rows, quarter + channels, width), bf16),
        ],
        scalars=1,
        inputs=4,
    )(strip_scalar, gathered, residual, weight, turned)

    returned = [results[0]]
    for ahead in range(1, strips):
        pairs = [(i, (i + ahead) % strips) for i in range(strips)]
        returned.append(lax.ppermute(results[ahead], "strip", pairs))

    by_chip = call(
        functools.partial(turn_body, quarter=quarter),
        jax.ShapeDtypeStruct((chips, chunk, LANES), bf16),
        scalars=1,
        inputs=2,
    )(core_scalar, kept, swapped)
    by_chip = exchange(by_chip, ("group", "line"))
    message = call(
        functools.partial(
            publish_body, quarter=quarter, capacity=capacity, groups=groups, cores=cores,
            root=root,
        ),
        jax.ShapeDtypeStruct((chips, chunk, LANES), bf16),
        scalars=1,
        inputs=2,
    )(strip_scalar, by_chip, slots)
    near = exchange(message, ("group", "line"))

    output, grad_input = call(
        functools.partial(collect_body, quarter=quarter),
        [jax.ShapeDtypeStruct((channels, width), bf16)] * 2,
        scalars=1,
        inputs=2 + strips,
    )(strip_scalar, pixels, upstream, *returned)

    far = lax.ppermute(near, "core", swap)
    owned_rows = call(
        functools.partial(owned_body, quarter=quarter, capacity=capacity, strips=strips),
        jax.ShapeDtypeStruct((cores * strips, capacity, padded), bf16),
    )(near)
    owned_rows = exchange(owned_rows, ("core", "strip"))
    new_weight = call(
        functools.partial(collect_weight_body, step=step),
        jax.ShapeDtypeStruct((quarter, taken), bf16),
        scalars=1,
        inputs=2,
    )(core_scalar, near, far)
    owned_rows, new_weight = lax.optimization_barrier((owned_rows, new_weight))
    new_master, new_first, new_second = call(
        functools.partial(finish_body, step=step, strips=strips, root=root),
        [jax.ShapeDtypeStruct(master.shape, f32)] * 3,
    )(owned_rows, master, first_moment, second_moment, filled)
    return (output[None, None], grad_input[None, None], new_weight, new_master, new_first, new_second)


def solution(mesh):
    fine = Mesh(
        mesh.devices.reshape(RANK_SHAPE + (mesh.shape["strip"],)),
        ("line", "group", "core", "strip"),
    )
    ranks = ("line", "group", "core")
    images = P(ranks, "strip", None, None)
    specs = (images, images, P("strip", None), P(ranks, None), P(ranks, None), P(ranks, None))

    return jax.shard_map(
        local, mesh=fine, in_specs=specs + (P(),), out_specs=specs, check_vma=False
    )
```

```python
import functools
import jax
import jax.numpy as jnp
from jax import lax
from jax.experimental import pallas as pl
from jax.experimental.pallas import tpu as pltpu
from jax.sharding import Mesh, PartitionSpec as P

beta_first = 0.9
beta_second = 0.999
learn_rate = 0.01
epsilon = 1e-08
bias_first = 1.0 - 0.9**10
bias_second = 1.0 - 0.999**10

interpret = False
LANES = 128
RANK_SHAPE = (8, 8, 2)
TERMS = 2
taps = [(dh, dw) for dh in (-1, 0, 1) for dw in (-1, 0, 1)]
f32 = jnp.float32
bf16 = jnp.bfloat16


def call(body, out_shape, scratch=(), scalars=0, inputs=0):
    specs = {}
    if scalars:
        specs["in_specs"] = [pl.BlockSpec(memory_space=pltpu.SMEM)] * scalars + [
            pl.BlockSpec(memory_space=pltpu.VMEM)
        ] * inputs
    return pl.pallas_call(
        body,
        out_shape=out_shape,
        scratch_shapes=scratch,
        interpret=interpret,
        compiler_params=pltpu.CompilerParams(vmem_limit_bytes=20 << 20),
        **specs,
    )


def dot(left, right, left_dim, right_dim):
    return lax.dot_general(
        left, right, (((left_dim,), (right_dim,)), ((), ())), preferred_element_type=f32
    )


def shifted(value):
    lane = lax.broadcasted_iota(jnp.int32, value.shape, 1)
    last = value.shape[1] - 1
    before = jnp.where(lane == 0, 0.0, pltpu.roll(value, 1, 1))
    after = jnp.where(lane == last, 0.0, pltpu.roll(value, last, 1))
    return {-1: before.astype(bf16), 0: value.astype(bf16), 1: after.astype(bf16)}


def fill(cols, rows, load, direction):
    first = load(0)
    count, width = first.shape
    for index, (dh, _) in enumerate(taps):
        for h in range(rows):
            if not 0 <= h + direction * dh < rows:
                cols[index * count : (index + 1) * count, h * width : (h + 1) * width] = jnp.zeros(
                    (count, width), bf16
                )
    for source in range(rows):
        versions = shifted(first if source == 0 else load(source))
        for index, (dh, dw) in enumerate(taps):
            h = source - direction * dh
            if 0 <= h < rows:
                cols[index * count : (index + 1) * count, h * width : (h + 1) * width] = versions[
                    direction * dw
                ]


def activated(gathered, channels, h):
    value = gathered[h, :channels, :].astype(f32)
    return (value / (1.0 + jnp.exp(-value))).astype(bf16).astype(f32)


def pack_body(pixels, upstream, outgoing, staged, arrived):
    strips, channels = outgoing.shape[0], pixels.shape[0]
    loads = [
        pltpu.make_async_copy(pixels, staged.at[:channels, :], arrived.at[0]),
        pltpu.make_async_copy(upstream, staged.at[channels:, :], arrived.at[1]),
    ]
    for load in loads:
        load.start()
    for load in loads:
        load.wait()
    quarter = channels // strips
    for strip in range(strips):
        outgoing[strip, :channels, :] = staged[:channels, :]
        outgoing[strip, channels:, :] = staged[
            channels + strip * quarter : channels + (strip + 1) * quarter, :
        ]


def split_body(master, first_moment, second_moment, pieces, *, step):
    state = jnp.concatenate([master[...], first_moment[...], second_moment[...]], axis=0)
    terms = []
    for _ in range(TERMS):
        term = state.astype(bf16).astype(f32)
        terms.append(term)
        state = state - term
    terms = jnp.concatenate(terms, axis=0)
    halves, height, padded = pieces.shape
    excess = (halves - 1) * step + padded - terms.shape[1]
    terms = jnp.concatenate([terms, jnp.zeros((height, excess), f32)], axis=1)
    for half in range(halves):
        pieces[half] = terms[:, half * step : half * step + padded].astype(bf16)


def gradient_body(core, gathered, pieces, target, cols, *, channels, step, other):
    rows = gathered.shape[0]
    quarter = gathered.shape[1] - channels
    fill(cols, rows, functools.partial(activated, gathered, channels), 1)
    whole = len(taps) * channels
    if cols.shape[0] > whole:
        cols[whole:, :] = jnp.zeros((cols.shape[0] - whole, cols.shape[1]), bf16)
    upstream = jnp.concatenate([gathered[h, channels:, :] for h in range(rows)], axis=1)
    half = 1 - core[0] if other else core[0]
    start = pl.multiple_of(half * step, 8)
    product = dot(upstream, cols[pl.ds(start, target.shape[1]), :], 1, 1)
    target[:quarter, :] = product.astype(bf16)
    target[quarter:, :] = pieces[half]


def convolution_body(
    strip, gathered, residual, weight, turned, *results, channels
):
    *results, cols, back_cols, whole = results
    rows, quarter, width = residual.shape
    fill(cols, rows, functools.partial(activated, gathered, channels), 1)
    convolved = dot(weight[...], cols[...], 1, 0)
    for h in range(rows):
        whole[h, :quarter, :] = (
            residual[h].astype(f32) + convolved[:, h * width : (h + 1) * width]
        ).astype(bf16)
    fill(back_cols, rows, lambda h: gathered[h, channels:, :].astype(f32), -1)
    spread = dot(turned[...], back_cols[...], 1, 0)
    for h in range(rows):
        whole[h, quarter:, :] = spread[:, h * width : (h + 1) * width].astype(bf16)
    for ahead, result in enumerate(results):
        target = strip[0] + ahead
        result[...] = whole[jnp.where(target >= rows, target - rows, target)]


def collect_body(strip, pixels, upstream, *pieces, quarter):
    *pieces, output, grad_input = pieces
    strips = len(pieces)
    spread = jnp.zeros(pixels.shape, f32)
    for behind, piece in enumerate(pieces):
        source = strip[0] - behind
        source = jnp.where(source < 0, source + strips, source)
        output[pl.ds(pl.multiple_of(source * quarter, quarter), quarter), :] = piece[:quarter, :]
        spread = spread + piece[quarter:, :].astype(f32)
    value = pixels[...].astype(f32)
    sigmoid = 1.0 / (1.0 + jnp.exp(-value))
    derivative = sigmoid * (1.0 + value * (1.0 - sigmoid))
    grad_input[...] = (upstream[...].astype(f32) + spread * derivative).astype(bf16)


def turn_body(core, kept, received, message, *, quarter):
    ours, others = kept[...].astype(f32), received[...].astype(f32)
    first = core[0] == 0
    rows = [
        ours[:quarter] + others[:quarter],
        jnp.where(first, ours[quarter:], others[quarter:]),
        jnp.where(first, others[quarter:], ours[quarter:]),
    ]
    spare = LANES - 2 * ours.shape[0] + quarter
    if spare:
        rows.append(jnp.zeros((spare, ours.shape[1]), f32))
    turned = jnp.transpose(jnp.concatenate(rows, axis=0))
    chips, chunk, _ = message.shape
    for chip in range(chips):
        message[chip] = turned[chip * chunk : (chip + 1) * chunk, :].astype(bf16)


def adam(grads, master, first_moment, second_moment):
    first_new = beta_first * first_moment + (1.0 - beta_first) * grads
    second_new = beta_second * second_moment + (1.0 - beta_second) * grads * grads
    update = learn_rate * (first_new / bias_first) / (jnp.sqrt(second_new / bias_second) + epsilon)
    return master - update, first_new, second_new


def publish_body(strip, received, slots, message, *, quarter, capacity, cores, root):
    chips, chunk, _ = received.shape
    strips = slots.shape[0]
    columns = max(LANES, chips * cores * capacity)
    mine = slots[0:1, :]
    for other in range(1, strips):
        mine = jnp.where(strip[0] == other, slots[other : other + 1, :], mine)
    wide = jnp.concatenate([mine] * 3, axis=1)
    owner, place = wide // capacity, wide % capacity
    share = TERMS * 3 * capacity
    row = lax.broadcasted_iota(jnp.int32, (LANES, 3 * LANES), 0) - quarter
    array = lax.broadcasted_iota(jnp.int32, (LANES, 3 * LANES), 1) // LANES
    within = row % (3 * capacity)
    here = (row >= 0) & (row < cores * share) & (wide >= 0) & (row // share == owner % cores)
    here = here & (within // capacity == array) & (within % capacity == place)
    here = jnp.where(here, 1.0, 0.0).astype(bf16)
    grads = jnp.sum(received[...].astype(f32), axis=0)
    picked = dot(rows_of(received), here, 1, 0)
    state = jnp.zeros((chunk, 3 * LANES), f32)
    for chip in range(chips):
        state = jnp.where(
            owner // cores == chip, picked[chip * chunk : (chip + 1) * chunk], state
        )
    fresh, _, _ = adam(
        grads / root, state[:, :LANES], state[:, LANES : 2 * LANES], state[:, 2 * LANES :]
    )
    index = lax.broadcasted_iota(jnp.int32, (columns, LANES), 0)
    matches = jnp.where(index == mine, 1.0, 0.0).astype(bf16)
    chosen = dot(grads.astype(bf16), matches, 1, 1)
    lane = lax.broadcasted_iota(jnp.int32, (chunk, LANES), 1)
    span = cores * capacity
    per_tile = LANES // span
    for chip in range(chips):
        tile = chosen[:, chip // per_tile * LANES : (chip // per_tile + 1) * LANES]
        shift = (quarter - span * (chip % per_tile)) % LANES
        moved = tile if shift == 0 else pltpu.roll(tile, shift, 1)
        value = jnp.where(lane < quarter, fresh, jnp.where(lane < quarter + span, moved, 0.0))
        message[chip] = value.astype(bf16)


def rows_of(messages):
    chips, chunk, _ = messages.shape
    return messages[...].reshape(chips * chunk, LANES)


def unit(rows, first):
    shape = (rows, LANES)
    row = lax.broadcasted_iota(jnp.int32, shape, 0)
    return jnp.where(row + first == lax.broadcasted_iota(jnp.int32, shape, 1), 1.0, 0.0).astype(
        bf16
    )


def owned_body(near, message, *, quarter, capacity, strips):
    targets = message.shape[0]
    turned = dot(unit(16, quarter), rows_of(near), 1, 1)
    for target in range(targets):
        first = target // strips * capacity
        message[target] = turned[first : first + capacity].astype(bf16)


def collect_weight_body(core, near, far, new_weight, *, step):
    ours, others = rows_of(near), rows_of(far)
    first = core[0] == 0
    rows = [jnp.where(first, ours, others)[:step], jnp.where(first, others, ours)[:step]]
    rows = jnp.concatenate(rows, axis=0)
    new_weight[...] = dot(unit(new_weight.shape[0], 0), rows, 1, 1).astype(bf16)


def finish_body(
    owned, master, first_moment, second_moment, filled,
    new_master, new_first, new_second, *, step, strips, root,
):
    halves = []
    for half in range(owned.shape[0] // strips):
        total = owned[half * strips].astype(f32)
        for strip in range(1, strips):
            total = total + owned[half * strips + strip].astype(f32)
        halves.append(total[:, :step])
    grads = jnp.concatenate(halves, axis=1) / root
    fresh, first_new, second_new = adam(
        grads, master[...], first_moment[...], second_moment[...]
    )
    keep = filled[...] > 0.0
    new_master[...] = jnp.where(keep, fresh, master[...])
    new_first[...] = jnp.where(keep, first_new, first_moment[...])
    new_second[...] = jnp.where(keep, second_new, second_moment[...])


def slot_tables(owner_list, capacity):
    count = owner_list.shape[0]
    same_owner = owner_list[:, None] == owner_list[None, :]
    order = jnp.arange(count, dtype=jnp.int32)
    earlier = order[None, :] < order[:, None]
    return owner_list * capacity + jnp.sum((same_owner & earlier).astype(jnp.int32), axis=1)


def exchange(value, axes):
    return lax.all_to_all(value, axes, 0, 0, tiled=True)


def local(latents, cotangent, weight, master, first_moment, second_moment, owner_list):
    lines, groups, cores, strips = (lax.axis_size(a) for a in ("line", "group", "core", "strip"))
    chips = lines * groups
    ranks = chips * cores
    strip, core = lax.axis_index("strip"), lax.axis_index("core")
    rank = (lax.axis_index("line") * groups + lax.axis_index("group")) * cores + core
    strip_scalar = strip.reshape(1).astype(jnp.int32)
    core_scalar = core.reshape(1).astype(jnp.int32)
    swap = [(i, cores - 1 - i) for i in range(cores)]
    channels, width = latents.shape[2:]
    quarter = channels // strips
    capacity = master.shape[0]
    height = TERMS * 3 * capacity
    taken = len(taps) * channels
    step = taken // cores
    padded = -(-step // LANES) * LANES
    chunk = padded // chips
    rows = strips
    root = float(ranks * rows * width) ** 0.5
    pixels, upstream = latents[0, 0], cotangent[0, 0]

    outgoing = pl.pallas_call(
        pack_body,
        out_shape=jax.ShapeDtypeStruct((strips, channels + quarter, width), bf16),
        in_specs=[pl.BlockSpec(memory_space=pltpu.HBM)] * 2,
        scratch_shapes=[
            pltpu.VMEM((2 * channels, width), bf16),
            pltpu.SemaphoreType.DMA((2,)),
        ],
        name="pack",
        interpret=interpret,
        compiler_params=pltpu.CompilerParams(vmem_limit_bytes=60 << 20),
    )(pixels, upstream)
    gathered = exchange(outgoing, "strip")

    slot_ids = slot_tables(owner_list, capacity)
    slots = jnp.pad(
        slot_ids.reshape(strips, quarter), ((0, 0), (0, LANES - quarter)), constant_values=-1
    )
    owned = jnp.sum((owner_list == rank).astype(jnp.int32))
    filled = (jnp.arange(capacity, dtype=jnp.int32) < owned).astype(f32)[:, None]
    turned = weight.reshape(quarter, len(taps), channels).transpose(2, 1, 0)
    turned = turned.reshape(channels, len(taps) * quarter)
    pieces = call(
        functools.partial(split_body, step=step),
        jax.ShapeDtypeStruct((cores, height, padded), bf16),
    )(master, first_moment, second_moment)
    gathered, slots, filled, turned, pieces = lax.optimization_barrier(
        (gathered, slots, filled, turned, pieces)
    )

    sent, kept = (
        call(
            functools.partial(gradient_body, channels=channels, step=step, other=other),
            jax.ShapeDtypeStruct((quarter + height, padded), bf16),
            [pltpu.VMEM(((cores - 1) * step + padded, rows * width), bf16)],
            scalars=1,
            inputs=2,
        )(core_scalar, gathered, pieces)
        for other in (True, False)
    )
    swapped = lax.ppermute(sent, "core", swap)

    residual = lax.dynamic_slice_in_dim(gathered, strip * quarter, quarter, axis=1)
    results = call(
        functools.partial(convolution_body, channels=channels),
        [jax.ShapeDtypeStruct((quarter + channels, width), bf16)] * strips,
        [
            pltpu.VMEM((taken, rows * width), bf16),
            pltpu.VMEM((len(taps) * quarter, rows * width), bf16),
            pltpu.VMEM((rows, quarter + channels, width), bf16),
        ],
        scalars=1,
        inputs=4,
    )(strip_scalar, gathered, residual, weight, turned)

    returned = [results[0]]
    for ahead in range(1, strips):
        pairs = [(i, (i + ahead) % strips) for i in range(strips)]
        returned.append(lax.ppermute(results[ahead], "strip", pairs))

    by_chip = call(
        functools.partial(turn_body, quarter=quarter),
        jax.ShapeDtypeStruct((chips, chunk, LANES), bf16),
        scalars=1,
        inputs=2,
    )(core_scalar, kept, swapped)
    by_chip = exchange(by_chip, ("line", "group"))
    message = call(
        functools.partial(publish_body, quarter=quarter, capacity=capacity, cores=cores, root=root),
        jax.ShapeDtypeStruct((chips, chunk, LANES), bf16),
        scalars=1,
        inputs=2,
    )(strip_scalar, by_chip, slots)
    near = exchange(message, ("line", "group"))

    output, grad_input = call(
        functools.partial(collect_body, quarter=quarter),
        [jax.ShapeDtypeStruct((channels, width), bf16)] * 2,
        scalars=1,
        inputs=2 + strips,
    )(strip_scalar, pixels, upstream, *returned)

    far = lax.ppermute(near, "core", swap)
    owned_rows = call(
        functools.partial(owned_body, quarter=quarter, capacity=capacity, strips=strips),
        jax.ShapeDtypeStruct((cores * strips, capacity, padded), bf16),
    )(near)
    owned_rows = exchange(owned_rows, ("core", "strip"))
    new_weight = call(
        functools.partial(collect_weight_body, step=step),
        jax.ShapeDtypeStruct((quarter, taken), bf16),
        scalars=1,
        inputs=2,
    )(core_scalar, near, far)
    owned_rows, new_weight = lax.optimization_barrier((owned_rows, new_weight))
    new_master, new_first, new_second = call(
        functools.partial(finish_body, step=step, strips=strips, root=root),
        [jax.ShapeDtypeStruct(master.shape, f32)] * 3,
    )(owned_rows, master, first_moment, second_moment, filled)
    return (output[None, None], grad_input[None, None], new_weight, new_master, new_first, new_second)


def solution(mesh):
    fine = Mesh(
        mesh.devices.reshape(RANK_SHAPE + (mesh.shape["strip"],)),
        ("line", "group", "core", "strip"),
    )
    ranks = ("line", "group", "core")
    images = P(ranks, "strip", None, None)
    specs = (images, images, P("strip", None), P(ranks, None), P(ranks, None), P(ranks, None))

    return jax.shard_map(
        local, mesh=fine, in_specs=specs + (P(),), out_specs=specs, check_vma=False
    )
```
